32 devices in a mesh: groups: 1, req: 32 (over z, y, x, core).
Axes of the slice: x: 2, y: 2, z: 4, core: 2. Of those that a mesh axis runs over, the one named last changes fastest.
Arguments:
- hidden: bfloat16 [2, 512, 2880], P(None, ('groups', 'req')), may hold values from -6 to 6
- norm_gain: bfloat16 [2880], replicated, may hold values from 0.099609375 to 1.8984375
- w_gate: bfloat16 [2880, 23040], P(None, 'req'), may hold values from -0.109375 to 0.109375
- w_up: bfloat16 [2880, 23040], P(None, 'req'), may hold values from -0.109375 to 0.109375
- w_down: bfloat16 [23040, 2880], P('req'), may hold values from -0.109375 to 0.109375
- expert_ids: int32 [2, 512, 4], P(None, ('groups', 'req')), may hold values from 0 to 7, as said below
- route_weight: float32 [2, 512, 4], P(None, ('groups', 'req')), may hold values from 0.1 to 1
Outputs:
- mixed: bfloat16 [2, 512, 2880], P(None, ('groups', 'req'))
The draws below stay inside these ranges and needn't reach their ends.
Inputs may be any that keep to these rules, and one draw needn't show every extreme that they name: `expert_ids`: each token names 4 different experts. In each micro-batch the 16 tokens of one device name any one expert at most 12 times, and every expert is named exactly 12 times by the tokens of some device.
All inputs are finite; a program needn't handle non-finite values.
Results may differ from the reference program's by a relative error of at most 0.0058.
Values may be sent and summed in bfloat16 or wider, within the bound.
A program may use at most 128 MiB of HBM per device.

```python
import math
import jax
import jax.numpy as jnp
from jax import lax

D = 2880
FF = 2880
TOP = 4
MICRO = 2
MB_TOK = 16
EXPERTS = 8
CAP = 12
TOKENS = 512
N_REQ = 32


def draw_expert_ids(key, part):
    remaining = MB_TOK * TOP - CAP
    cycle = max(TOP, (remaining + CAP - 1) // CAP)
    flat = jnp.arange(MB_TOK * TOP, dtype=jnp.int32)
    token_pos = flat // TOP
    member = flat % TOP
    is_own = (member == 0) & (token_pos < CAP)
    before = jnp.minimum(CAP, (flat + TOP - 1) // TOP)
    ranked = flat - before

    def one_device(batch_index, device_index):
        device_key = jax.random.fold_in(jax.random.fold_in(key, 7919 + batch_index), device_index)
        own_expert = device_index % EXPERTS
        others = (own_expert + 1 + jax.random.permutation(device_key, EXPERTS - 1).astype(jnp.int32)) % EXPERTS
        picked = others[ranked % cycle]
        return jnp.where(is_own, own_expert, picked).astype(jnp.int32).reshape(MB_TOK, TOP)
    batches = jnp.arange(MICRO, dtype=jnp.int32)
    devices_all = jnp.arange(N_REQ, dtype=jnp.int32)
    table = jax.vmap(lambda batch_index: jax.vmap(lambda device_index: one_device(batch_index, device_index))(devices_all))(batches)
    return table.reshape(MICRO, TOKENS, TOP).astype(jnp.int32)


def level_of(rng, shape, pieces, low, high):
    gain, own = 1.0, jax.random.fold_in(rng, 6)
    for dim, blocks in pieces:
        steps = jnp.exp(jax.random.uniform(jax.random.fold_in(own, dim), (blocks,), jnp.float32, low / len(pieces), high / len(pieces)))
        gain = gain * jnp.repeat(steps, shape[dim] // blocks).reshape([-1 if axis == dim else 1 for axis in range(len(shape))])
    return gain


def gaussian(key, extent, spread, bound, pieces=(), held_as=jnp.bfloat16):
    level = level_of(key, extent, pieces, -0.22, 0.18) if pieces else 1.0
    values = jax.random.normal(key, extent, jnp.float32) * spread * level
    return jnp.minimum(jnp.maximum(values, -bound), bound).astype(held_as)


def setup_inputs(seed: int = 0, part: int = 0) -> dict:
    streams_of = jax.random.split(jax.random.key(seed), 8)
    part_splits = jax.random.split(jax.random.fold_in(streams_of[7], part), 8)
    hidden = gaussian(part_splits[0], (MICRO, TOKENS, D), 1.0, 6.0, ((1, 32),))
    norm_gain = jnp.clip(1.0 + 0.18 * jax.random.normal(streams_of[1], (D,), jnp.float32), 0.099609375, 1.8984375).astype(jnp.bfloat16)
    w_gate = gaussian(streams_of[2], (D, EXPERTS * FF), D ** -0.5, 0.109375, ((1, 32),))
    w_up = gaussian(streams_of[3], (D, EXPERTS * FF), D ** -0.5, 0.109375, ((1, 32),))
    w_down = gaussian(streams_of[4], (EXPERTS * FF, D), FF ** -0.5, 0.109375, ((0, 32),))
    expert_ids = draw_expert_ids(jax.random.fold_in(jax.random.fold_in(streams_of[7], part), 71), part)
    route_weight = jnp.clip(jnp.exp(math.log(1.0) - 2.3025851 * jax.random.uniform(part_splits[6], (MICRO, TOKENS, TOP), jnp.float32) ** level_of(part_splits[6], (MICRO, TOKENS, TOP), ((1, 32),), -0.2, 0.2)), 0.1, 1.0)
    return {"hidden": hidden, "norm_gain": norm_gain, "w_gate": w_gate, "w_up": w_up, "w_down": w_down, "expert_ids": expert_ids, "route_weight": route_weight}


epsilon = 1e-05
swish_scale = 1.702

def one_batch(hidden_rows, norm_gain, w_gate, w_up, w_down, chosen, weighing):
    residual = hidden_rows.astype(jnp.float32)
    normed = (residual * lax.rsqrt(lax.optimization_barrier(jnp.mean(residual * residual, axis=-1, keepdims=True)) + epsilon) * norm_gain.astype(jnp.float32)).astype(jnp.bfloat16)
    blocks = chosen.reshape(N_REQ, MB_TOK * TOP)
    onehot = (blocks[:, :, None] == jnp.arange(EXPERTS, dtype=jnp.int32)[None, None, :]).astype(jnp.int32)
    slot_index = lax.optimization_barrier(jnp.sum((jnp.cumsum(onehot, axis=1) - onehot) * onehot, axis=-1))
    source = jnp.broadcast_to(jnp.arange(N_REQ, dtype=jnp.int32)[:, None], blocks.shape)
    row_index = ((blocks * N_REQ + source) * CAP + slot_index).reshape(-1).astype(jnp.int32)
    token_of = (jnp.arange(TOKENS * TOP, dtype=jnp.int32) // TOP).astype(jnp.int32)
    buffer = jnp.zeros((EXPERTS * N_REQ * CAP, D), jnp.bfloat16).at[row_index].set(normed[token_of])
    buffer = buffer.reshape(EXPERTS, N_REQ * CAP, D)

    def run_expert(expert):
        slot_rows = buffer[expert]
        start = (expert * FF).astype(jnp.int32)
        gate_cols = lax.dynamic_slice_in_dim(w_gate, start, FF, 1)
        up_cols = lax.dynamic_slice_in_dim(w_up, start, FF, 1)
        down_rows = lax.dynamic_slice_in_dim(w_down, start, FF, 0)
        gate = jnp.dot(slot_rows, gate_cols, preferred_element_type=jnp.float32)
        upward = jnp.dot(slot_rows, up_cols, preferred_element_type=jnp.float32)
        act = ((upward + 1.0) * gate * jax.nn.sigmoid(swish_scale * gate)).astype(jnp.bfloat16)
        return jnp.dot(act, down_rows, preferred_element_type=jnp.float32).astype(jnp.bfloat16)
    outputs = lax.map(run_expert, jnp.arange(EXPERTS, dtype=jnp.int32))
    gathered = outputs.reshape(-1, D)[row_index].reshape(TOKENS, TOP, D).astype(jnp.float32)
    combined = residual
    for member in range(TOP):
        combined = combined + weighing[:, member, None] * gathered[:, member]
    return combined.astype(jnp.bfloat16)

def reference(hidden, norm_gain, w_gate, w_up, w_down, expert_ids, route_weight):
    results = []
    for batch_index in range(MICRO):
        results.append(one_batch(hidden[batch_index], norm_gain, w_gate, w_up, w_down, expert_ids[batch_index], route_weight[batch_index]))
    return jnp.stack(results, axis=0)
```

```python
import functools

import jax
import jax.numpy as jnp
from jax import lax
from jax.experimental import pallas as pl
from jax.experimental.pallas import tpu as pltpu
from jax.sharding import PartitionSpec as P

HSPLIT = 4


epsilon = 1e-05
swish_scale = 1.702


def swapped(block, axis, apart):
    count = lax.axis_size(axis)
    route = []
    for low in range(count):
        high = low | 1 << apart
        if high != low and high < count:
            route += [(low, high), (high, low)]
    return lax.ppermute(block, axis, route)


def routed_local(hidden, norm_gain, w_gate, w_up, w_down, expert_ids, route_weight):
    micro_count, tokens, model_width = hidden.shape
    top_count = expert_ids.shape[2]
    devices = lax.axis_size("req")
    experts = devices // HSPLIT
    rounded = HSPLIT * (
        (3 * tokens * top_count + 2 * experts * HSPLIT - 1) // (2 * experts * HSPLIT)
    )
    capacity = min(tokens, max(HSPLIT, rounded))
    quarter = capacity // HSPLIT
    levels = HSPLIT.bit_length() - 1
    position = lax.axis_index("req")
    gain_f32 = norm_gain.astype(jnp.float32)
    results = []
    for batch_index in range(micro_count):
        residual = hidden[batch_index].astype(jnp.float32)
        normed = (
            residual
            * lax.rsqrt(jnp.mean(residual * residual, axis=-1, keepdims=True) + epsilon)
            * gain_f32
        ).astype(jnp.bfloat16)
        flat_ids = expert_ids[batch_index].reshape(-1)
        onehot = (flat_ids[:, None] == jnp.arange(experts, dtype=jnp.int32)[None, :]).astype(
            jnp.int32
        )
        slot_index = jnp.sum((jnp.cumsum(onehot, axis=0) - onehot) * onehot, axis=1)
        target = flat_ids * capacity + slot_index
        placing = (
            target[:, None] == jnp.arange(experts * capacity, dtype=jnp.int32)[None, :]
        ).reshape(tokens, top_count, experts * capacity)
        selector = jnp.any(placing, axis=1).astype(jnp.bfloat16)
        outgoing = jnp.dot(selector.T, normed, preferred_element_type=jnp.float32).astype(
            jnp.bfloat16
        )
        copies = jnp.broadcast_to(
            outgoing.reshape(experts, 1, capacity, model_width),
            (experts, HSPLIT, capacity, model_width),
        ).reshape(devices, capacity, model_width)
        received = lax.all_to_all(copies, "req", split_axis=0, concat_axis=0, tiled=True)
        count = received.shape[1]
        slot_rows = received.reshape(-1, model_width)
        gate = jnp.dot(slot_rows, w_gate, preferred_element_type=jnp.float32)
        upward = jnp.dot(slot_rows, w_up, preferred_element_type=jnp.float32)
        act = ((upward + 1.0) * gate * jax.nn.sigmoid(swish_scale * gate)).astype(jnp.bfloat16)
        source_form = jnp.dot(act, w_down, preferred_element_type=jnp.float32).reshape(
            devices, count, model_width
        )
        shard_form = source_form.reshape(devices, HSPLIT, quarter, model_width).transpose(
            1, 0, 2, 3
        )
        folded = shard_form
        for bit_index in reversed(range(levels)):
            halfway = folded.shape[0] // 2
            upper_side = position >> bit_index & 1 == 1
            kept_part = jnp.where(upper_side, folded[halfway:], folded[:halfway])
            given_part = jnp.where(upper_side, folded[:halfway], folded[halfway:])
            folded = kept_part + swapped(given_part, "req", bit_index)
        own_rows = folded[0].astype(jnp.bfloat16)
        expert_out = lax.all_to_all(
            own_rows, "req", split_axis=0, concat_axis=0, tiled=True
        ).reshape(experts * capacity, model_width)
        weigh_table = jnp.sum(
            placing.astype(jnp.float32) * route_weight[batch_index][:, :, None], axis=1
        )
        mixture = jnp.dot(
            weigh_table, expert_out.astype(jnp.float32), precision=lax.Precision.HIGHEST
        )
        results.append((residual + mixture).astype(jnp.bfloat16))
    return jnp.stack(results, axis=0)

LANES = 128
PLANES = 4
CORE, X, Y, Z = 1, 2, 4, 8
SHARES = ((8, "zyx"), (10, "zxy"), (5, "yxz"))
VMEM_BYTES = 60 * 1024 * 1024
LINK_RATE, CORE_RATE = 47.5e3, 350e3
CORE_DELAY, HOP_DELAY, FURTHER_DELAY = 1.0, 1.7, 0.8
UP_SPAN, DOWN_SPAN, ADD_SPAN, STEP_SPAN = 0.9, 0.5, 0.01, 0.02
ROW = slice(0, 1)
PAIR = slice(0, 2)


def padded(size):
    return -(-size // LANES) * LANES


def lane_streams(width):
    tiles, total, low, streams = width // LANES, sum(share for share, _ in SHARES), 0, []
    for number, (share, order) in enumerate(SHARES):
        taken = sum(part for part, _ in SHARES[: number + 1])
        high = tiles * taken // total * LANES
        streams.append((low, high, order))
        low = high
    return streams


def one(value):
    return slice(value, value + 1)


def block(order, first, second, depth):
    return (first, second, depth) if order == "zyx" else (second, first, depth)


def gather_messages(order):
    every, later = slice(0, PLANES), slice(1, PLANES)
    own = (ROW, ROW, ROW)
    messages = []
    if order == "yxz":
        square = (PAIR, PAIR, ROW)
        messages += [
            ("y0", Y, own, ()),
            ("x0", X, own, ()),
            ("xy", X, (ROW, one(1), ROW), ("y0",)),
            ("z2", 2 * Z, square, ("x0", "xy")),
            ("z1", Z, square, ("x0", "xy")),
            ("z3", Z, (PAIR, PAIR, one(2)), ("z2",)),
            ("c0", CORE, square, ("x0", "xy")),
            ("c2", CORE, (PAIR, PAIR, one(2)), ("z2",)),
            ("c1", CORE, (PAIR, PAIR, one(1)), ("z1",)),
            ("c3", CORE, (PAIR, PAIR, one(3)), ("z3",)),
        ]
        return messages
    far, near = (X, Y) if order == "zyx" else (Y, X)
    planes = tuple("z%d" % plane for plane in range(1, PLANES))
    messages += [("z%d" % plane, plane * Z, own, ()) for plane in range(1, PLANES)]
    messages += [
        ("n0", near, own, ()),
        ("f0", far, own, ()),
        ("nz", near, (ROW, ROW, later), planes),
        ("fz", far, (ROW, ROW, later), planes),
        ("fn", far, block(order, ROW, one(1), ROW), ("n0",)),
        ("fnz", far, block(order, ROW, one(1), later), ("nz",)),
        ("c0", CORE, own, ()),
        ("cz", CORE, (ROW, ROW, later), planes),
        ("cn", CORE, block(order, ROW, one(1), every), ("n0", "nz")),
        ("cf", CORE, block(order, one(1), ROW, every), ("f0", "fz")),
        ("cfn", CORE, block(order, one(1), one(1), every), ("fn", "fnz")),
    ]
    return messages


def reduce_steps(order):
    every, later = slice(0, PLANES), slice(1, PLANES)
    own = (ROW, ROW, ROW)
    if order == "yxz":
        at = lambda plane: (PAIR, PAIR, one(plane))
        return [
            (at(3), [("z3", Z, at(3))], []),
            (at(1), [("z1", Z, at(1))], []),
            (at(2), [("z2", 2 * Z, at(2))], [("z3", at(3))]),
            (
                (one(1), PAIR, ROW),
                [("x", X, (one(1), PAIR, ROW))],
                [("z1", (one(1), PAIR, one(1))), ("z2", (one(1), PAIR, one(2)))],
            ),
            (
                (ROW, one(1), ROW),
                [("y", Y, (ROW, one(1), ROW))],
                [
                    ("z1", (ROW, one(1), one(1))),
                    ("z2", (ROW, one(1), one(2))),
                    ("x", (one(1), one(1), ROW)),
                ],
            ),
            (
                own,
                [],
                [
                    ("z1", (ROW, ROW, one(1))),
                    ("z2", (ROW, ROW, one(2))),
                    ("x", (one(1), ROW, ROW)),
                    ("y", (ROW, one(1), ROW)),
                ],
            ),
        ]
    far, near = (X, Y) if order == "zyx" else (Y, X)
    at = functools.partial(block, order)
    corner, side, face = at(one(1), one(1), every), at(one(1), ROW, every), at(ROW, one(1), every)
    planes = [(ROW, ROW, one(plane)) for plane in range(1, PLANES)]
    names = ["z%d" % plane for plane in range(1, PLANES)]
    return [
        (corner, [("fn", far, corner)], []),
        (side, [("f", far, side)], []),
        (face, [("n", near, face)], [("fn", corner)]),
        (
            (ROW, ROW, later),
            [(name, plane * Z, planes[plane - 1]) for plane, name in enumerate(names, 1)],
            [("f", at(one(1), ROW, later)), ("n", at(ROW, one(1), later))],
        ),
        (
            own,
            [],
            [("f", at(one(1), ROW, ROW)), ("n", at(ROW, one(1), ROW))] + list(zip(names, planes)),
        ),
    ]


def rows_of(rows):
    return [
        (x, y, z)
        for x in range(rows[0].start, rows[0].stop)
        for y in range(rows[1].start, rows[1].stop)
        for z in range(rows[2].start, rows[2].stop)
    ]


def lane_pieces(low, high, size):
    return [(start, min(high, start + size)) for start in range(low, high, size)]


def all_actions(micro_count, tokens, width, model_width, ups):
    streams = lane_streams(width)
    actions = []
    for batch in range(micro_count):
        for number, (low, high, order) in enumerate(streams):
            for name, hop, rows, needs in gather_messages(order):
                label = ("g", batch, number, name)
                needed = [("g", batch, number, need) for need in needs]
                if batch and not needs:
                    needed = [("s", batch - 1, 0, "fz"), ("s", batch - 1, 1, "fz")]
                size = 2 * len(rows_of(rows)) * tokens * (high - low)
                actions.append((("s", batch, number, name), needed, STEP_SPAN, [(label, hop, size)]))
    for batch in range(micro_count):
        for number, (low, high, order) in enumerate(streams):
            for index, (rows, sends, arrived) in enumerate(reduce_steps(order)):
                needed = [("d", batch, number, 0), ("r", batch, number, "c")]
                needed += [("r", batch, number, name) for name, _ in arrived]
                count = len(rows_of(rows))
                made = [
                    (("r", batch, number, name), hop, 2 * len(rows_of(sent)) * tokens * (high - low))
                    for name, hop, sent in sends
                ]
                span = STEP_SPAN + ADD_SPAN * count * (2 + len(arrived)) * (high - low) / 1024
                actions.append((("a", batch, number, index), needed, span, made))
    for batch in range(micro_count):
        done = []
        for side in (0, 1):
            for piece in range(len(ups)):
                needed = [
                    ("g", batch, number, name)
                    for number, (_, _, order) in enumerate(streams)
                    for name, hop, _, _ in gather_messages(order)
                    if (hop == CORE) == bool(side)
                ]
                actions.append((("u", batch, side, piece), needed + done[-1:], UP_SPAN, []))
                done.append(("u", batch, side, piece))
        for number, (low, high, order) in enumerate(streams):
            for side in (1, 0):
                made = []
                if side:
                    size = 2 * PLANES * 4 * tokens * (high - low)
                    made = [(("r", batch, number, "c"), CORE, size)]
                span = DOWN_SPAN * (high - low) / 1024
                actions.append((("d", batch, number, side), done[-1:], span, made))
                done.append(("d", batch, number, side))
    return actions


def plan_actions(actions):
    moment, ready_at, link_free, order = 0.0, {}, {}, []
    left = list(actions)
    while left:
        best = None
        for action in left:
            if all(need in ready_at for need in action[1]):
                start = max([ready_at[need] for need in action[1]], default=0.0)
                if start <= moment:
                    best = (moment, action)
                    break
                if best is None or start < best[0]:
                    best = (start, action)
        start, action = best
        left.remove(action)
        order.append(action)
        moment = max(moment, start) + action[2]
        ready_at[action[0]] = moment
        for label, hop, size in action[3]:
            link = "z" if hop >= Z else hop
            rate = CORE_RATE if hop == CORE else LINK_RATE
            delay = CORE_DELAY if hop == CORE else HOP_DELAY + FURTHER_DELAY * (hop > Z)
            link_free[link] = max(link_free.get(link, 0.0), moment) + size / rate
            ready_at[label] = link_free[link] + delay
    return order, moment


def tree_kernel(
    hidden_ref,
    gain_ref,
    ids_ref,
    weight_ref,
    gate_hbm,
    up_hbm,
    down_hbm,
    out_ref,
    rows,
    parts,
    arrived,
    gate_w,
    up_w,
    down_w,
    act,
    weight_sems,
    send_sems,
    recv_sems,
):
    micro_count, tokens, model_width = hidden_ref.shape
    width = rows.shape[-1]
    devices = lax.axis_size("req")
    group = devices // 2
    me = lax.axis_index("req")
    experts = devices // HSPLIT
    expert = me // HSPLIT
    streams = lane_streams(width)
    hops = [CORE, X, Y] + [plane * Z for plane in range(1, PLANES)]

    def across(hop):
        if hop < Z:
            return me + (1 - 2 * ((me // hop) % 2)) * hop
        plane, flips = me // Z, hop // Z
        low = plane % 2 + (flips % 2) * (1 - 2 * (plane % 2))
        high = plane // 2 + (flips // 2) * (1 - 2 * (plane // 2))
        return me % Z + Z * (2 * high + low)

    partner = {hop: across(hop) for hop in hops}
    barrier = pltpu.get_barrier_semaphore()
    for hop in hops:
        pl.semaphore_signal(
            barrier, inc=1, device_id={"req": partner[hop]}, device_id_type=pl.DeviceIdType.MESH
        )
    loads = [
        pltpu.make_async_copy(source, target, weight_sems.at[number])
        for number, (source, target) in enumerate(
            ((gate_hbm, gate_w), (up_hbm, up_w), (down_hbm, down_w))
        )
    ]
    for load in loads:
        load.start()

    tail = width - model_width
    lane_of = lax.broadcasted_iota(jnp.int32, (1, tail), 1)
    gain = gain_ref[...].astype(jnp.float32)
    for batch in range(micro_count):
        residual = hidden_ref[batch].astype(jnp.float32)
        scale = lax.rsqrt(jnp.mean(residual * residual, axis=-1, keepdims=True) + epsilon)
        rows[batch, 0, 0, 0, 0, :, :model_width] = (residual * scale * gain).astype(jnp.bfloat16)
        named = lane_of - experts * (lane_of // experts)
        table = jnp.zeros((tokens, tail), jnp.float32)
        for member in range(ids_ref.shape[2]):
            table = table + jnp.where(
                ids_ref[batch, :, member : member + 1] == named,
                weight_ref[batch, :, member : member + 1],
                0.0,
            )
        upper = table.astype(jnp.bfloat16).astype(jnp.float32)
        shown = jnp.where(lane_of < experts, upper, table - upper)
        shown = jnp.where(lane_of < 2 * experts, shown, 0.0)
        rows[batch, 0, 0, 0, 0, :, model_width:] = shown.astype(jnp.bfloat16)
    pl.semaphore_wait(barrier, len(hops))

    slots = {}

    def remote(source, target, label, hop):
        number = slots.setdefault(label, len(slots))
        return pltpu.make_async_remote_copy(
            src_ref=source,
            dst_ref=target,
            send_sem=send_sems.at[number],
            recv_sem=recv_sems.at[number],
            device_id={"req": partner[hop]},
            device_id_type=pl.DeviceIdType.MESH,
        )

    copies = {}
    for batch in range(micro_count):
        for number, (low, high, order) in enumerate(streams):
            lanes = slice(low, high)
            for name, hop, (xs, ys, zs), _ in gather_messages(order):
                flip = lambda part, bit: one(part.start ^ 1) if hop == bit else part
                landing = (flip(xs, X), flip(ys, Y), zs)
                if hop >= Z:
                    landing = (xs, ys, one(zs.start ^ (hop // Z)))
                side = 1 if hop == CORE else 0
                label = ("g", batch, number, name)
                copies[label] = remote(
                    rows.at[batch, 0, xs, ys, zs, :, lanes],
                    rows.at[(batch, side) + landing + (slice(None), lanes)],
                    label,
                    hop,
                )
            label = ("r", batch, number, "c")
            copies[label] = remote(
                parts.at[batch, 1, :, :, :, :, lanes],
                arrived.at[batch, 1, :, :, :, :, lanes],
                label,
                CORE,
            )
            for _, sends, _ in reduce_steps(order):
                for name, hop, (xs, ys, zs) in sends:
                    label = ("r", batch, number, name)
                    copies[label] = remote(
                        parts.at[batch, 0, xs, ys, zs, :, lanes],
                        arrived.at[batch, 0, xs, ys, zs, :, lanes],
                        label,
                        hop,
                    )

    chosen = (lane_of == expert) | (lane_of == experts + expert)
    hidden_units = gate_w.shape[0]
    ups = lane_pieces(0, hidden_units, 256)
    rowwise = (((1,), (1,)), ((), ()))

    def up_piece(batch, side, piece):
        low, high = ups[piece]
        slab = rows[batch, side, :, :, :, :, :model_width].reshape(group * tokens, model_width)
        gate = lax.dot_general(
            slab, gate_w[low:high, :], rowwise, preferred_element_type=jnp.float32
        )
        upward = lax.dot_general(
            slab, up_w[low:high, :], rowwise, preferred_element_type=jnp.float32
        )
        act[side, :, low:high] = (
            (upward + 1.0) * gate * jax.nn.sigmoid(swish_scale * gate)
        ).astype(jnp.bfloat16)

    def down_piece(batch, number, side):
        low, high, _ = streams[number]
        ends = rows[batch, side, :, :, :, :, model_width:].reshape(group * tokens, tail)
        weight = jnp.sum(jnp.where(chosen, ends.astype(jnp.float32), 0.0), axis=1, keepdims=True)
        for start, stop in lane_pieces(low, min(high, model_width), 512):
            part = jnp.dot(
                act[side], down_w[:, start:stop], preferred_element_type=jnp.float32
            )
            parts[batch, side, :, :, :, :, start:stop] = (
                (part * weight).astype(parts.dtype).reshape(2, 2, PLANES, tokens, stop - start)
            )

    def reduce_piece(batch, number, index):
        low, high, order = streams[number]
        target, sends, others = reduce_steps(order)[index]
        stop = high if sends else min(high, model_width)
        held = rows_of(target)
        for place, (x, y, z) in enumerate(held):
            total = parts[batch, 0, x, y, z, :, low:stop].astype(jnp.float32)
            if not sends:
                total = total + hidden_ref[batch, :, low:stop].astype(jnp.float32)
            total = total + arrived[batch, 1, x, y, z, :, low:stop].astype(jnp.float32)
            for _, block_rows in others:
                inside = rows_of(block_rows)
                matching = inside if len(held) == 1 else [inside[place]]
                for ox, oy, oz in matching:
                    total = total + arrived[batch, 0, ox, oy, oz, :, low:stop].astype(jnp.float32)
            if sends:
                parts[batch, 0, x, y, z, :, low:stop] = total.astype(parts.dtype)
            else:
                out_ref[batch, :, low:stop] = total.astype(out_ref.dtype)

    parts[:, :, :, :, :, :, model_width:] = jnp.zeros(parts.shape[:-1] + (tail,), parts.dtype)
    landed, loaded = set(), set()
    actions = all_actions(micro_count, tokens, width, model_width, ups)
    for key, needs, _, sends in plan_actions(actions)[0]:
        for need in needs:
            if need in copies and need not in landed:
                landed.add(need)
                copies[need].wait_recv()
        kind, batch, number, index = key
        if kind == "u":
            if kind not in loaded:
                loads[0].wait()
                loads[1].wait()
            up_piece(batch, number, index)
        elif kind == "d":
            if kind not in loaded:
                loads[2].wait()
            down_piece(batch, number, index)
        elif kind == "a":
            reduce_piece(batch, number, index)
        loaded.add(kind)
        for label, _, _ in sends:
            copies[label].start()
    for label, copy in copies.items():
        if label not in landed:
            copy.wait_recv()
        copy.wait_send()


def tree_local(hidden, norm_gain, w_gate, w_up, w_down, expert_ids, route_weight):
    micro_count, tokens, model_width = hidden.shape
    devices = lax.axis_size("req")
    width = padded(model_width)
    hidden_units = w_gate.shape[1]
    vmem = pl.BlockSpec(memory_space=pltpu.VMEM)
    hbm = pl.BlockSpec(memory_space=pl.ANY)
    slots = (micro_count, 2, 2, 2, PLANES, tokens, width)
    messages = micro_count * sum(
        1 + len(gather_messages(order)) + sum(len(step[1]) for step in reduce_steps(order))
        for _, _, order in lane_streams(width)
    )
    return pl.pallas_call(
        tree_kernel,
        out_shape=jax.ShapeDtypeStruct(hidden.shape, hidden.dtype),
        in_specs=[vmem, vmem, vmem, vmem, hbm, hbm, hbm],
        out_specs=vmem,
        scratch_shapes=[
            pltpu.VMEM(slots, jnp.bfloat16),
            pltpu.VMEM(slots, jnp.bfloat16),
            pltpu.VMEM(slots, jnp.bfloat16),
            pltpu.VMEM((hidden_units, model_width), w_gate.dtype),
            pltpu.VMEM((hidden_units, model_width), w_up.dtype),
            pltpu.VMEM((hidden_units, model_width), w_down.dtype),
            pltpu.VMEM((2, devices // 2 * tokens, hidden_units), jnp.bfloat16),
            pltpu.SemaphoreType.DMA((3,)),
            pltpu.SemaphoreType.DMA((messages,)),
            pltpu.SemaphoreType.DMA((messages,)),
        ],
        compiler_params=pltpu.CompilerParams(
            collective_id=0, has_side_effects=True, vmem_limit_bytes=VMEM_BYTES
        ),
        name="tree",
    )(hidden, norm_gain[None, :], expert_ids, route_weight, w_gate.T, w_up.T, w_down)


def tree_fits(hidden, norm_gain, w_gate, w_up, w_down, expert_ids, route_weight):
    micro_count, tokens, model_width = hidden.shape
    devices = lax.axis_size("req")
    width = padded(model_width)
    units = w_gate.shape[1]
    slots = 3 * micro_count * devices * tokens * width
    weights = 3 * units * width
    work = 3 * devices * tokens * width
    return (
        devices == 8 * PLANES
        and 2 * (devices // HSPLIT) <= width - model_width
        and 2 * (slots + weights + work) <= VMEM_BYTES
    )


def local(*arguments):
    return (tree_local if tree_fits(*arguments) else routed_local)(*arguments)


def solution(mesh):
    return jax.shard_map(
        local,
        mesh=mesh,
        in_specs=(
            P(None, ("groups", "req"), None),
            P(),
            P(None, "req"),
            P(None, "req"),
            P("req", None),
            P(None, ("groups", "req"), None),
            P(None, ("groups", "req"), None),
        ),
        out_specs=P(None, ("groups", "req"), None),
        check_vma=False,
    )
```

```python
import functools

import jax
import jax.numpy as jnp
from jax import lax
from jax.experimental import pallas as pl
from jax.experimental.pallas import tpu as pltpu
from jax.sharding import PartitionSpec as P

HSPLIT = 4


epsilon = 1e-05
swish_scale = 1.702


def swapped(block, axis, apart):
    count = lax.axis_size(axis)
    route = []
    for low in range(count):
        high = low | 1 << apart
        if high != low and high < count:
            route += [(low, high), (high, low)]
    return lax.ppermute(block, axis, route)


def routed_local(hidden, norm_gain, w_gate, w_up, w_down, expert_ids, route_weight):
    micro_count, tokens, model_width = hidden.shape
    top_count = expert_ids.shape[2]
    devices = lax.axis_size("req")
    experts = devices // HSPLIT
    rounded = HSPLIT * (
        (3 * tokens * top_count + 2 * experts * HSPLIT - 1) // (2 * experts * HSPLIT)
    )
    capacity = min(tokens, max(HSPLIT, rounded))
    quarter = capacity // HSPLIT
    levels = HSPLIT.bit_length() - 1
    position = lax.axis_index("req")
    gain_f32 = norm_gain.astype(jnp.float32)
    results = []
    for batch_index in range(micro_count):
        residual = hidden[batch_index].astype(jnp.float32)
        normed = (
            residual
            * lax.rsqrt(jnp.mean(residual * residual, axis=-1, keepdims=True) + epsilon)
            * gain_f32
        ).astype(jnp.bfloat16)
        flat_ids = expert_ids[batch_index].reshape(-1)
        onehot = (flat_ids[:, None] == jnp.arange(experts, dtype=jnp.int32)[None, :]).astype(
            jnp.int32
        )
        slot_index = jnp.sum((jnp.cumsum(onehot, axis=0) - onehot) * onehot, axis=1)
        target = flat_ids * capacity + slot_index
        placing = (
            target[:, None] == jnp.arange(experts * capacity, dtype=jnp.int32)[None, :]
        ).reshape(tokens, top_count, experts * capacity)
        selector = jnp.any(placing, axis=1).astype(jnp.bfloat16)
        outgoing = jnp.dot(selector.T, normed, preferred_element_type=jnp.float32).astype(
            jnp.bfloat16
        )
        copies = jnp.broadcast_to(
            outgoing.reshape(experts, 1, capacity, model_width),
            (experts, HSPLIT, capacity, model_width),
        ).reshape(devices, capacity, model_width)
        received = lax.all_to_all(copies, "req", split_axis=0, concat_axis=0, tiled=True)
        count = received.shape[1]
        slot_rows = received.reshape(-1, model_width)
        gate = jnp.dot(slot_rows, w_gate, preferred_element_type=jnp.float32)
        upward = jnp.dot(slot_rows, w_up, preferred_element_type=jnp.float32)
        act = ((upward + 1.0) * gate * jax.nn.sigmoid(swish_scale * gate)).astype(jnp.bfloat16)
        source_form = jnp.dot(act, w_down, preferred_element_type=jnp.float32).reshape(
            devices, count, model_width
        )
        shard_form = source_form.reshape(devices, HSPLIT, quarter, model_width).transpose(
            1, 0, 2, 3
        )
        folded = shard_form
        for bit_index in reversed(range(levels)):
            halfway = folded.shape[0] // 2
            upper_side = position >> bit_index & 1 == 1
            kept_part = jnp.where(upper_side, folded[halfway:], folded[:halfway])
            given_part = jnp.where(upper_side, folded[:halfway], folded[halfway:])
            folded = kept_part + swapped(given_part, "req", bit_index)
        own_rows = folded[0].astype(jnp.bfloat16)
        expert_out = lax.all_to_all(
            own_rows, "req", split_axis=0, concat_axis=0, tiled=True
        ).reshape(experts * capacity, model_width)
        weigh_table = jnp.sum(
            placing.astype(jnp.float32) * route_weight[batch_index][:, :, None], axis=1
        )
        mixture = jnp.dot(
            weigh_table, expert_out.astype(jnp.float32), precision=lax.Precision.HIGHEST
        )
        results.append((residual + mixture).astype(jnp.bfloat16))
    return jnp.stack(results, axis=0)

LANES = 128
PLANES = 4
CORE, X, Y, Z = 1, 2, 4, 8
GROUPS = (
    ((3, "zyx"), (3, "zxy")),
    ((2, "yxz"), (3, "zxy"), (4, "zyx")),
    ((4, "yxz"), (4, "zyx")),
)
PREFERENCE = {
    ("s", 0): 0,
    ("s", 1): 1,
    ("a", 0): 0,
    ("a", 1): 1,
    ("u", 0): 3,
    ("u", 1): 4,
    ("d", 0): 2,
    ("d", 1): 5,
}
SHARES = tuple(stream for members in GROUPS for stream in members)
HELD = 1
VMEM_BYTES = 60 * 1024 * 1024
LINK_RATE, CORE_RATE = 48.5e3, 570e3
LINKS = {
    CORE: (((CORE, 1),), 1.06),
    X: (((X, 1),), 1.86),
    Y: (((Y, 1),), 1.86),
    Z: (((Z, 1),), 1.86),
    2 * Z: (((Z, 1), (2 * Z, 2)), 2.66),
    3 * Z: (((Z, 1), (2 * Z, 2)), 3.41),
}
UP_SPAN, DOWN_SPAN, ADD_SPAN, STEP_SPAN = 2.96, 0.7, 0.0116, 0.085
ROW = slice(0, 1)
PAIR = slice(0, 2)


def padded(size):
    return -(-size // LANES) * LANES


def lane_streams(width):
    tiles, total, low, streams = width // LANES, sum(share for share, _ in SHARES), 0, []
    for number, (share, order) in enumerate(SHARES):
        taken = sum(part for part, _ in SHARES[: number + 1])
        high = tiles * taken // total * LANES
        streams.append((low, high, order))
        low = high
    return streams


def one(value):
    return slice(value, value + 1)


def block(order, first, second, depth):
    return (first, second, depth) if order == "zyx" else (second, first, depth)


def gather_messages(order):
    every, later = slice(0, PLANES), slice(1, PLANES)
    own = (ROW, ROW, ROW)
    messages = []
    if order == "yxz":
        square = (PAIR, PAIR, ROW)
        messages += [
            ("y0", Y, own, ()),
            ("x0", X, own, ()),
            ("xy", X, (ROW, one(1), ROW), ("y0",)),
            ("z2", 2 * Z, square, ("x0", "xy")),
            ("z1", Z, square, ("x0", "xy")),
            ("z3", Z, (PAIR, PAIR, one(2)), ("z2",)),
            ("c", CORE, (PAIR, PAIR, every), ("x0", "xy", "z1", "z2", "z3")),
        ]
        return messages
    far, near = (X, Y) if order == "zyx" else (Y, X)
    planes = tuple("z%d" % plane for plane in range(1, PLANES))
    messages += [("z%d" % plane, plane * Z, own, ()) for plane in range(1, PLANES)]
    messages += [
        ("n0", near, own, ()),
        ("f0", far, own, ()),
        ("nz", near, (ROW, ROW, later), planes),
        ("fz", far, (ROW, ROW, later), planes),
        ("fn", far, block(order, ROW, one(1), ROW), ("n0",)),
        ("fnz", far, block(order, ROW, one(1), later), ("nz",)),
        ("c", CORE, (PAIR, PAIR, every), ("f0", "fz", "fn", "fnz")),
    ]
    return messages


def reduce_steps(order):
    every, later = slice(0, PLANES), slice(1, PLANES)
    own = (ROW, ROW, ROW)
    if order == "yxz":
        at = lambda plane: (PAIR, PAIR, one(plane))
        return [
            (at(3), [("z3", Z, at(3))], []),
            (at(1), [("z1", Z, at(1))], []),
            (at(2), [("z2", 2 * Z, at(2))], [("z3", at(3))]),
            (
                (one(1), PAIR, ROW),
                [("x", X, (one(1), PAIR, ROW))],
                [("z1", (one(1), PAIR, one(1))), ("z2", (one(1), PAIR, one(2)))],
            ),
            (
                (ROW, one(1), ROW),
                [("y", Y, (ROW, one(1), ROW))],
                [
                    ("z1", (ROW, one(1), one(1))),
                    ("z2", (ROW, one(1), one(2))),
                    ("x", (one(1), one(1), ROW)),
                ],
            ),
            (
                own,
                [],
                [
                    ("z1", (ROW, ROW, one(1))),
                    ("z2", (ROW, ROW, one(2))),
                    ("x", (one(1), ROW, ROW)),
                    ("y", (ROW, one(1), ROW)),
                ],
            ),
        ]
    far, near = (X, Y) if order == "zyx" else (Y, X)
    at = functools.partial(block, order)
    corner, side, face = at(one(1), one(1), every), at(one(1), ROW, every), at(ROW, one(1), every)
    planes = [(ROW, ROW, one(plane)) for plane in range(1, PLANES)]
    names = ["z%d" % plane for plane in range(1, PLANES)]
    return [
        (corner, [("fn", far, corner)], []),
        (side, [("f", far, side)], []),
        (face, [("n", near, face)], [("fn", corner)]),
        (
            (ROW, ROW, later),
            [(name, plane * Z, planes[plane - 1]) for plane, name in enumerate(names, 1)],
            [("f", at(one(1), ROW, later)), ("n", at(ROW, one(1), later))],
        ),
        (
            own,
            [],
            [("f", at(one(1), ROW, ROW)), ("n", at(ROW, one(1), ROW))] + list(zip(names, planes)),
        ),
    ]


def together(label, order):
    kind, _, _, name = label
    planes = ("z1", "z2", "z3")
    if order != "yxz" and name in planes:
        return planes, (ROW, ROW, slice(1, PLANES))
    if kind == "g" and order == "yxz" and name in ("x0", "xy"):
        return ("x0", "xy"), (one(1), PAIR, ROW)
    if kind == "g" and order != "yxz" and name in ("f0", "fz", "fn", "fnz"):
        return ("f0", "fz", "fn", "fnz"), block(order, one(1), PAIR, slice(0, PLANES))
    return None


def rows_of(rows):
    return [
        (x, y, z)
        for x in range(rows[0].start, rows[0].stop)
        for y in range(rows[1].start, rows[1].stop)
        for z in range(rows[2].start, rows[2].stop)
    ]


def lane_pieces(low, high, size):
    return [(start, min(high, start + size)) for start in range(low, high, size)]


def group_streams(group):
    first = sum(len(members) for members in GROUPS[:group])
    return range(first, first + len(GROUPS[group]))


def all_actions(micro_count, tokens, width, ups):
    streams = lane_streams(width)
    whole = 2 * PLANES * 4 * tokens
    actions = []
    for batch in range(micro_count):
        for number, (low, high, order) in enumerate(streams):
            for name, hop, rows, needs in gather_messages(order):
                needed = [("g", batch, number, need) for need in needs]
                if batch and not needs:
                    needed = [("s", batch - 1, HELD, gather_messages(streams[HELD][2])[-2][0])]
                made = [(("g", batch, number, name), hop, rows, low, high)]
                actions.append((("s", batch, number, name), needed, STEP_SPAN, made))
    for batch in range(micro_count):
        for number, (low, high, order) in enumerate(streams):
            group = [number in group_streams(index) for index in range(len(GROUPS))].index(True)
            for index, (rows, sends, arrived) in enumerate(reduce_steps(order)):
                needed = [("d", batch, group, 0), ("r", batch, number, "c")]
                needed += [("r", batch, number, name) for name, _ in arrived]
                made = [
                    (("r", batch, number, name), hop, sent, low, high) for name, hop, sent in sends
                ]
                count = len(rows_of(rows)) * (2 + len(arrived))
                span = STEP_SPAN + ADD_SPAN * count * (high - low) / 1024
                actions.append((("a", batch, number, index), needed, span, made))
    every = (PAIR, PAIR, slice(0, PLANES))
    for batch in range(micro_count):
        before = [("d", batch - 1, group, side) for group in range(len(GROUPS)) for side in (0, 1)]
        before = before if batch else []
        for group in range(len(GROUPS)):
            numbers = group_streams(group)
            share = sum(streams[number][1] - streams[number][0] for number in numbers) / width
            for side in (0, 1):
                needed = [
                    ("g", batch, number, name)
                    for number in numbers
                    for name, hop, _, _ in gather_messages(streams[number][2])
                    if (hop == CORE) == bool(side)
                ]
                for piece in range(len(ups)):
                    earlier = [("u", batch, group - 1, side, piece)] if group else before
                    span = UP_SPAN * share / len(ups)
                    actions.append((("u", batch, group, side, piece), needed + earlier, span, []))
        done = [
            ("u", batch, len(GROUPS) - 1, side, piece) for side in (0, 1) for piece in range(len(ups))
        ]
        for group in range(len(GROUPS)):
            numbers = group_streams(group)
            share = sum(streams[number][1] - streams[number][0] for number in numbers) / width
            for side in (1, 0):
                made = [
                    (("r", batch, number, "c"), CORE, every) + streams[number][:2]
                    for number in numbers
                    if side
                ]
                actions.append((("d", batch, group, side), done, DOWN_SPAN * share, made))
                done = done + [("d", batch, group, side)]
    return actions


def plan_actions(actions, tokens):
    moment, ready_at, link_free, order = 0.0, {}, {}, []
    left = sorted(
        actions,
        key=lambda action: (PREFERENCE[action[0][:2]], {"s": 0, "a": 0}.get(action[0][0], 0) * action[0][2]),
    )
    while left:
        best = None
        for action in left:
            if all(need in ready_at for need in action[1]):
                start = max([ready_at[need] for need in action[1]], default=0.0)
                if start <= moment:
                    best = (moment, action)
                    break
                if best is None or start < best[0]:
                    best = (start, action)
        start, action = best
        left.remove(action)
        order.append(action)
        moment = max(moment, start) + action[2]
        ready_at[action[0]] = moment
        for label, hop, rows, low, high in action[3]:
            span = 2 * len(rows_of(rows)) * tokens * (high - low)
            span = span / (CORE_RATE if hop == CORE else LINK_RATE)
            used, delay = LINKS[hop]
            for link, times in used:
                link_free[link] = max(link_free.get(link, 0.0), moment) + span * times
            ready_at[label] = max(link_free[link] for link, _ in used) + delay
    return order, moment


def tree_kernel(
    hidden_ref,
    gain_ref,
    ids_ref,
    weight_ref,
    gate_hbm,
    up_hbm,
    down_hbm,
    out_ref,
    rows,
    parts,
    arrived,
    gate_w,
    up_w,
    down_w,
    act,
    gate_part,
    up_part,
    weight_sems,
    send_sem,
    recv_sems,
    sent,
):
    micro_count, tokens, model_width = hidden_ref.shape
    width = rows.shape[-1]
    devices = lax.axis_size("req")
    half = devices // 2
    me = lax.axis_index("req")
    experts = devices // HSPLIT
    expert = me // HSPLIT
    streams = lane_streams(width)
    hops = [CORE, X, Y] + [plane * Z for plane in range(1, PLANES)]

    def across(hop):
        if hop < Z:
            return me + (1 - 2 * ((me // hop) % 2)) * hop
        plane, flips = me // Z, hop // Z
        low = plane % 2 + (flips % 2) * (1 - 2 * (plane % 2))
        high = plane // 2 + (flips // 2) * (1 - 2 * (plane // 2))
        return me % Z + Z * (2 * high + low)

    partner = {hop: across(hop) for hop in hops}
    barrier = pltpu.get_barrier_semaphore()
    for hop in hops:
        pl.semaphore_signal(
            barrier, inc=1, device_id={"req": partner[hop]}, device_id_type=pl.DeviceIdType.MESH
        )
    loads = [
        pltpu.make_async_copy(source, target, weight_sems.at[number])
        for number, (source, target) in enumerate(
            ((gate_hbm, gate_w), (up_hbm, up_w), (down_hbm, down_w))
        )
    ]
    for load in loads:
        load.start()

    tail = width - model_width
    lane_of = lax.broadcasted_iota(jnp.int32, (1, tail), 1)
    line_of = lax.broadcasted_iota(jnp.int32, (tail, 1), 0)
    named = line_of - experts * (line_of // experts)
    gain = gain_ref[...].astype(jnp.float32)[None, :]
    for batch in range(micro_count):
        residual = hidden_ref[batch].astype(jnp.float32)
        scale = lax.rsqrt(jnp.mean(residual * residual, axis=-1, keepdims=True) + epsilon)
        rows[batch, 0, 0, 0, 0, :, :model_width] = (residual * scale * gain).astype(jnp.bfloat16)
        table = jnp.zeros((tail, tokens), jnp.float32)
        for member in range(ids_ref.shape[1]):
            table = table + jnp.where(
                ids_ref[batch, member : member + 1, :] == named,
                weight_ref[batch, member : member + 1, :],
                0.0,
            )
        table = table.T
        upper = table.astype(jnp.bfloat16).astype(jnp.float32)
        shown = jnp.where(lane_of < experts, upper, table - upper)
        shown = jnp.where(lane_of < 2 * experts, shown, 0.0)
        rows[batch, 0, 0, 0, 0, :, model_width:] = shown.astype(jnp.bfloat16)
    pl.semaphore_wait(barrier, len(hops))

    slots = {}
    waits = {}

    def remote(source, target, label, hop):
        kind, batch, number, name = label
        low, high, order = streams[number]
        taken = together(label, order)
        key = label if taken is None else label[:3] + taken[0]
        slot = slots.setdefault(key, len(slots))
        copy = pltpu.make_async_remote_copy(
            src_ref=source,
            dst_ref=target,
            send_sem=send_sem,
            recv_sem=recv_sems.at[slot],
            device_id={"req": partner[hop]},
            device_id_type=pl.DeviceIdType.MESH,
        )
        if taken is None:
            waits[label] = (key, copy.wait_recv)
        else:
            xs, ys, zs = taken[1]
            whole = (rows if kind == "g" else arrived).at[batch, 0, xs, ys, zs, :, low:high]
            waits[label] = (key, pltpu.make_async_copy(whole, whole, recv_sems.at[slot]).wait)
        return copy

    copies = {}
    for batch in range(micro_count):
        for number, (low, high, order) in enumerate(streams):
            lanes = slice(low, high)
            for name, hop, (xs, ys, zs), _ in gather_messages(order):
                flip = lambda part, bit: one(part.start ^ 1) if hop == bit else part
                landing = (flip(xs, X), flip(ys, Y), zs)
                if hop >= Z:
                    landing = (xs, ys, one(zs.start ^ (hop // Z)))
                side = 1 if hop == CORE else 0
                label = ("g", batch, number, name)
                copies[label] = remote(
                    rows.at[batch, 0, xs, ys, zs, :, lanes],
                    rows.at[(batch, side) + landing + (slice(None), lanes)],
                    label,
                    hop,
                )
            label = ("r", batch, number, "c")
            copies[label] = remote(
                parts.at[batch, 1, :, :, :, :, lanes],
                arrived.at[batch, 1, :, :, :, :, lanes],
                label,
                CORE,
            )
            for _, sends, _ in reduce_steps(order):
                for name, hop, (xs, ys, zs) in sends:
                    label = ("r", batch, number, name)
                    copies[label] = remote(
                        parts.at[batch, 0, xs, ys, zs, :, lanes],
                        arrived.at[batch, 0, xs, ys, zs, :, lanes],
                        label,
                        hop,
                    )

    chosen = (lane_of == expert) | (lane_of == experts + expert)
    hidden_units = gate_w.shape[0]
    ups = lane_pieces(0, hidden_units, 256)
    rowwise = (((1,), (1,)), ((), ()))

    def up_piece(batch, group, side, piece):
        low, high = ups[piece]
        numbers = group_streams(group)
        start, stop = streams[numbers[0]][0], min(streams[numbers[-1]][1], model_width)
        slab = rows[batch, side, :, :, :, :, start:stop].reshape(half * tokens, stop - start)
        gate = lax.dot_general(
            slab, gate_w[low:high, start:stop], rowwise, preferred_element_type=jnp.float32
        )
        upward = lax.dot_general(
            slab, up_w[low:high, start:stop], rowwise, preferred_element_type=jnp.float32
        )
        if group:
            gate = gate_part[side, :, low:high] + gate
            upward = up_part[side, :, low:high] + upward
        if group < len(GROUPS) - 1:
            gate_part[side, :, low:high] = gate
            up_part[side, :, low:high] = upward
        else:
            act[side, :, low:high] = (
                (upward + 1.0) * gate * jax.nn.sigmoid(swish_scale * gate)
            ).astype(jnp.bfloat16)

    def down_piece(batch, group, side):
        numbers = group_streams(group)
        low, high = streams[numbers[0]][0], min(streams[numbers[-1]][1], model_width)
        ends = rows[batch, side, :, :, :, :, model_width:].reshape(half * tokens, tail)
        weight = jnp.sum(jnp.where(chosen, ends.astype(jnp.float32), 0.0), axis=1, keepdims=True)
        for start, stop in lane_pieces(low, high, 512):
            part = jnp.dot(
                act[side], down_w[:, start:stop], preferred_element_type=jnp.float32
            )
            parts[batch, side, :, :, :, :, start:stop] = (
                (part * weight).astype(parts.dtype).reshape(2, 2, PLANES, tokens, stop - start)
            )

    def reduce_piece(batch, number, index):
        low, high, order = streams[number]
        target, sends, others = reduce_steps(order)[index]
        stop = high if sends else min(high, model_width)
        held = rows_of(target)
        for place, (x, y, z) in enumerate(held):
            total = parts[batch, 0, x, y, z, :, low:stop].astype(jnp.float32)
            if not sends:
                total = total + hidden_ref[batch, :, low:stop].astype(jnp.float32)
            total = total + arrived[batch, 1, x, y, z, :, low:stop].astype(jnp.float32)
            for _, block_rows in others:
                inside = rows_of(block_rows)
                matching = inside if len(held) == 1 else [inside[place]]
                for ox, oy, oz in matching:
                    total = total + arrived[batch, 0, ox, oy, oz, :, low:stop].astype(jnp.float32)
            if sends:
                parts[batch, 0, x, y, z, :, low:stop] = total.astype(parts.dtype)
            else:
                out_ref[batch, :, low:stop] = total.astype(out_ref.dtype)

    parts[:, :, :, :, :, :, model_width:] = jnp.zeros(parts.shape[:-1] + (tail,), parts.dtype)
    landed, loaded = set(), set()
    actions = all_actions(micro_count, tokens, width, ups)
    for key, needs, _, sends in plan_actions(actions, tokens)[0]:
        for need in needs:
            if need in waits and waits[need][0] not in landed:
                landed.add(waits[need][0])
                waits[need][1]()
        kind = key[0]
        if kind == "u":
            if kind not in loaded:
                loads[0].wait()
                loads[1].wait()
            up_piece(*key[1:])
        elif kind == "d":
            if kind not in loaded:
                loads[2].wait()
            down_piece(*key[1:])
        elif kind == "a":
            reduce_piece(*key[1:])
        loaded.add(kind)
        for label, *_ in sends:
            copies[label].start()
    pltpu.make_async_copy(sent, sent, send_sem).wait()


def tree_local(hidden, norm_gain, w_gate, w_up, w_down, expert_ids, route_weight):
    micro_count, tokens, model_width = hidden.shape
    devices = lax.axis_size("req")
    width = padded(model_width)
    hidden_units = w_gate.shape[1]
    vmem = pl.BlockSpec(memory_space=pltpu.VMEM)
    hbm = pl.BlockSpec(memory_space=pl.ANY)
    slots = (micro_count, 2, 2, 2, PLANES, tokens, width)
    labels = [
        (kind, batch, number, name)
        for batch in range(micro_count)
        for number, (_, _, order) in enumerate(lane_streams(width))
        for kind, names in (
            ("g", [message[0] for message in gather_messages(order)]),
            ("r", ["c"] + [name for step in reduce_steps(order) for name, _, _ in step[1]]),
        )
        for name in names
    ]
    orders = [order for _, _, order in lane_streams(width)]
    grouped = [together(label, orders[label[2]]) for label in labels]
    messages = len(
        {
            label if taken is None else label[:3] + taken[0]
            for label, taken in zip(labels, grouped)
        }
    )
    return pl.pallas_call(
        tree_kernel,
        out_shape=jax.ShapeDtypeStruct(hidden.shape, hidden.dtype),
        in_specs=[vmem, vmem, vmem, vmem, hbm, hbm, hbm],
        out_specs=vmem,
        scratch_shapes=[
            pltpu.VMEM(slots, jnp.bfloat16),
            pltpu.VMEM(slots, jnp.bfloat16),
            pltpu.VMEM(slots, jnp.bfloat16),
            pltpu.VMEM((hidden_units, model_width), w_gate.dtype),
            pltpu.VMEM((hidden_units, model_width), w_up.dtype),
            pltpu.VMEM((hidden_units, model_width), w_down.dtype),
            pltpu.VMEM((2, devices // 2 * tokens, hidden_units), jnp.bfloat16),
            pltpu.VMEM((2, devices // 2 * tokens, hidden_units), jnp.float32),
            pltpu.VMEM((2, devices // 2 * tokens, hidden_units), jnp.float32),
            pltpu.SemaphoreType.DMA((3,)),
            pltpu.SemaphoreType.DMA,
            pltpu.SemaphoreType.DMA((messages,)),
            pltpu.VMEM((2 * micro_count * (devices - 1), tokens, width), jnp.bfloat16),
        ],
        compiler_params=pltpu.CompilerParams(
            collective_id=0, has_side_effects=True, vmem_limit_bytes=VMEM_BYTES
        ),
        name="tree",
    )(
        hidden,
        norm_gain,
        expert_ids.transpose(0, 2, 1),
        route_weight.transpose(0, 2, 1),
        w_gate.T,
        w_up.T,
        w_down,
    )


def tree_fits(hidden, norm_gain, w_gate, w_up, w_down, expert_ids, route_weight):
    micro_count, tokens, model_width = hidden.shape
    devices = lax.axis_size("req")
    width = padded(model_width)
    units = w_gate.shape[1]
    slots = 3 * micro_count * devices * tokens * width
    weights = 3 * units * width
    work = 3 * devices * tokens * width
    return (
        devices == 8 * PLANES
        and 2 * (devices // HSPLIT) <= width - model_width
        and 2 * (slots + weights + work) <= VMEM_BYTES
    )


def local(*arguments):
    return (tree_local if tree_fits(*arguments) else routed_local)(*arguments)


def solution(mesh):
    return jax.shard_map(
        local,
        mesh=mesh,
        in_specs=(
            P(None, ("groups", "req"), None),
            P(),
            P(None, "req"),
            P(None, "req"),
            P("req", None),
            P(None, ("groups", "req"), None),
            P(None, ("groups", "req"), None),
        ),
        out_specs=P(None, ("groups", "req"), None),
        check_vma=False,
    )
```

```python
import functools

import jax
import jax.numpy as jnp
from jax import lax
from jax.experimental import pallas as pl
from jax.experimental.pallas import tpu as pltpu
from jax.sharding import PartitionSpec as P

HSPLIT = 4


epsilon = 1e-05
swish_scale = 1.702


def swapped(block, axis, apart):
    count = lax.axis_size(axis)
    route = []
    for low in range(count):
        high = low | 1 << apart
        if high != low and high < count:
            route += [(low, high), (high, low)]
    return lax.ppermute(block, axis, route)


def routed_local(hidden, norm_gain, w_gate, w_up, w_down, expert_ids, route_weight):
    micro_count, tokens, model_width = hidden.shape
    top_count = expert_ids.shape[2]
    devices = lax.axis_size("req")
    experts = devices // HSPLIT
    rounded = HSPLIT * (
        (3 * tokens * top_count + 2 * experts * HSPLIT - 1) // (2 * experts * HSPLIT)
    )
    capacity = min(tokens, max(HSPLIT, rounded))
    quarter = capacity // HSPLIT
    levels = HSPLIT.bit_length() - 1
    position = lax.axis_index("req")
    gain_f32 = norm_gain.astype(jnp.float32)
    results = []
    for batch_index in range(micro_count):
        residual = hidden[batch_index].astype(jnp.float32)
        normed = (
            residual
            * lax.rsqrt(jnp.mean(residual * residual, axis=-1, keepdims=True) + epsilon)
            * gain_f32
        ).astype(jnp.bfloat16)
        flat_ids = expert_ids[batch_index].reshape(-1)
        onehot = (flat_ids[:, None] == jnp.arange(experts, dtype=jnp.int32)[None, :]).astype(
            jnp.int32
        )
        slot_index = jnp.sum((jnp.cumsum(onehot, axis=0) - onehot) * onehot, axis=1)
        target = flat_ids * capacity + slot_index
        placing = (
            target[:, None] == jnp.arange(experts * capacity, dtype=jnp.int32)[None, :]
        ).reshape(tokens, top_count, experts * capacity)
        selector = jnp.any(placing, axis=1).astype(jnp.bfloat16)
        outgoing = jnp.dot(selector.T, normed, preferred_element_type=jnp.float32).astype(
            jnp.bfloat16
        )
        copies = jnp.broadcast_to(
            outgoing.reshape(experts, 1, capacity, model_width),
            (experts, HSPLIT, capacity, model_width),
        ).reshape(devices, capacity, model_width)
        received = lax.all_to_all(copies, "req", split_axis=0, concat_axis=0, tiled=True)
        count = received.shape[1]
        slot_rows = received.reshape(-1, model_width)
        gate = jnp.dot(slot_rows, w_gate, preferred_element_type=jnp.float32)
        upward = jnp.dot(slot_rows, w_up, preferred_element_type=jnp.float32)
        act = ((upward + 1.0) * gate * jax.nn.sigmoid(swish_scale * gate)).astype(jnp.bfloat16)
        source_form = jnp.dot(act, w_down, preferred_element_type=jnp.float32).reshape(
            devices, count, model_width
        )
        shard_form = source_form.reshape(devices, HSPLIT, quarter, model_width).transpose(
            1, 0, 2, 3
        )
        folded = shard_form
        for bit_index in reversed(range(levels)):
            halfway = folded.shape[0] // 2
            upper_side = position >> bit_index & 1 == 1
            kept_part = jnp.where(upper_side, folded[halfway:], folded[:halfway])
            given_part = jnp.where(upper_side, folded[:halfway], folded[halfway:])
            folded = kept_part + swapped(given_part, "req", bit_index)
        own_rows = folded[0].astype(jnp.bfloat16)
        expert_out = lax.all_to_all(
            own_rows, "req", split_axis=0, concat_axis=0, tiled=True
        ).reshape(experts * capacity, model_width)
        weigh_table = jnp.sum(
            placing.astype(jnp.float32) * route_weight[batch_index][:, :, None], axis=1
        )
        mixture = jnp.dot(
            weigh_table, expert_out.astype(jnp.float32), precision=lax.Precision.HIGHEST
        )
        results.append((residual + mixture).astype(jnp.bfloat16))
    return jnp.stack(results, axis=0)

LANES = 128
PLANES = 4
CORE, X, Y, Z = 1, 2, 4, 8
GROUPS = (
    ((6, "zxy"), (4, "zyx")),
    ((5, "yxz"), (3, "zyx")),
    ((5, "zxy"),),
)
PREFERENCE = {
    ("s", 0): 0,
    ("s", 1): 2,
    ("a", 0): 0,
    ("a", 1): 1,
    ("u", 0): 4,
    ("u", 1): 5,
    ("d", 0): 3,
    ("d", 1): 6,
}
SHARES = tuple(stream for members in GROUPS for stream in members)
HELD = 3
VMEM_BYTES = 60 * 1024 * 1024
LINK_RATE, CORE_RATE = 49.5e3, 1400e3
LINKS = {
    CORE: (((CORE, 1),), 1.12),
    X: (((X, 1),), 1.92),
    Y: (((Y, 1),), 1.92),
    Z: (((Z, 1),), 1.92),
    2 * Z: (((Z, 1), (2 * Z, 2)), 2.72),
    3 * Z: (((Z, 1), (2 * Z, 2)), 3.47),
}
UP_SPAN, DOWN_SPAN, DOWN_START, ADD_SPAN = 2.58, 1.33, 0.08, 0.0144
STEP_SPAN, SEND_SPAN, MESSAGE_SPAN = 0.092, 0.023, 0.034
ROW = slice(0, 1)
PAIR = slice(0, 2)


def padded(size):
    return -(-size // LANES) * LANES


def lane_streams(width):
    tiles, total, low, streams = width // LANES, sum(share for share, _ in SHARES), 0, []
    for number, (share, order) in enumerate(SHARES):
        taken = sum(part for part, _ in SHARES[: number + 1])
        high = tiles * taken // total * LANES
        streams.append((low, high, order))
        low = high
    return streams


def one(value):
    return slice(value, value + 1)


def block(order, first, second, depth):
    return (first, second, depth) if order == "zyx" else (second, first, depth)


def gather_messages(order):
    every, later = slice(0, PLANES), slice(1, PLANES)
    own = (ROW, ROW, ROW)
    messages = []
    if order == "yxz":
        square = (PAIR, PAIR, ROW)
        messages += [
            ("y0", Y, own, ()),
            ("x0", X, own, ()),
            ("xy", X, (ROW, one(1), ROW), ("y0",)),
            ("z2", 2 * Z, square, ("x0", "xy")),
            ("z1", Z, square, ("x0", "xy")),
            ("z3", Z, (PAIR, PAIR, one(2)), ("z2",)),
            ("c", CORE, (PAIR, PAIR, every), ("x0", "xy", "z1", "z2", "z3")),
        ]
        return messages
    far, near = (X, Y) if order == "zyx" else (Y, X)
    planes = tuple("z%d" % plane for plane in range(1, PLANES))
    messages += [("z%d" % plane, plane * Z, own, ()) for plane in range(1, PLANES)]
    messages += [
        ("n0", near, own, ()),
        ("f0", far, own, ()),
        ("nz", near, (ROW, ROW, later), planes),
        ("fz", far, (ROW, ROW, later), planes),
        ("fn", far, block(order, ROW, one(1), ROW), ("n0",)),
        ("fnz", far, block(order, ROW, one(1), later), ("nz",)),
        ("c", CORE, (PAIR, PAIR, every), ("f0", "fz", "fn", "fnz")),
    ]
    return messages


def reduce_steps(order):
    every, later = slice(0, PLANES), slice(1, PLANES)
    own = (ROW, ROW, ROW)
    if order == "yxz":
        at = lambda plane: (PAIR, PAIR, one(plane))
        return [
            (at(3), [("z3", Z, at(3))], []),
            (at(1), [("z1", Z, at(1))], []),
            (at(2), [("z2", 2 * Z, at(2))], [("z3", at(3))]),
            (
                (one(1), PAIR, ROW),
                [("x", X, (one(1), PAIR, ROW))],
                [("z1", (one(1), PAIR, one(1))), ("z2", (one(1), PAIR, one(2)))],
            ),
            (
                (ROW, one(1), ROW),
                [("y", Y, (ROW, one(1), ROW))],
                [
                    ("z1", (ROW, one(1), one(1))),
                    ("z2", (ROW, one(1), one(2))),
                    ("x", (one(1), one(1), ROW)),
                ],
            ),
            (
                own,
                [],
                [
                    ("z1", (ROW, ROW, one(1))),
                    ("z2", (ROW, ROW, one(2))),
                    ("x", (one(1), ROW, ROW)),
                    ("y", (ROW, one(1), ROW)),
                ],
            ),
        ]
    far, near = (X, Y) if order == "zyx" else (Y, X)
    at = functools.partial(block, order)
    corner, side, face = at(one(1), one(1), every), at(one(1), ROW, every), at(ROW, one(1), every)
    planes = [(ROW, ROW, one(plane)) for plane in range(1, PLANES)]
    names = ["z%d" % plane for plane in range(1, PLANES)]
    return [
        (corner, [("fn", far, corner)], []),
        (side, [("f", far, side)], []),
        (face, [("n", near, face)], [("fn", corner)]),
        (
            (ROW, ROW, later),
            [(name, plane * Z, planes[plane - 1]) for plane, name in enumerate(names, 1)],
            [("f", at(one(1), ROW, later)), ("n", at(ROW, one(1), later))],
        ),
        (
            own,
            [],
            [("f", at(one(1), ROW, ROW)), ("n", at(ROW, one(1), ROW))] + list(zip(names, planes)),
        ),
    ]


def together(label, order):
    kind, _, _, name = label
    planes = ("z1", "z2", "z3")
    if order != "yxz" and name in planes:
        return planes, (ROW, ROW, slice(1, PLANES))
    if kind == "g" and order == "yxz" and name in ("x0", "xy"):
        return ("x0", "xy"), (one(1), PAIR, ROW)
    if kind == "g" and order != "yxz" and name in ("f0", "fz", "fn", "fnz"):
        return ("f0", "fz", "fn", "fnz"), block(order, one(1), PAIR, slice(0, PLANES))
    return None


def rows_of(rows):
    return [
        (x, y, z)
        for x in range(rows[0].start, rows[0].stop)
        for y in range(rows[1].start, rows[1].stop)
        for z in range(rows[2].start, rows[2].stop)
    ]


def lane_pieces(low, high, size):
    return [(start, min(high, start + size)) for start in range(low, high, size)]


def group_streams(group):
    first = sum(len(members) for members in GROUPS[:group])
    return range(first, first + len(GROUPS[group]))


def all_actions(micro_count, tokens, width, ups):
    streams = lane_streams(width)
    whole = 2 * PLANES * 4 * tokens
    actions = []
    for batch in range(micro_count):
        for number, (low, high, order) in enumerate(streams):
            for name, hop, rows, needs in gather_messages(order):
                needed = [("g", batch, number, need) for need in needs]
                if batch and not needs:
                    needed = [("s", batch - 1, HELD, gather_messages(streams[HELD][2])[-2][0])]
                made = [(("g", batch, number, name), hop, rows, low, high)]
                actions.append((("s", batch, number, name), needed, STEP_SPAN, made))
    for batch in range(micro_count):
        for number, (low, high, order) in enumerate(streams):
            group = [number in group_streams(index) for index in range(len(GROUPS))].index(True)
            for index, (rows, sends, arrived) in enumerate(reduce_steps(order)):
                needed = [("d", batch, group, 0), ("r", batch, number, "c")]
                needed += [("r", batch, number, name) for name, _ in arrived]
                made = [
                    (("r", batch, number, name), hop, sent, low, high) for name, hop, sent in sends
                ]
                count = len(rows_of(rows)) * (2 + len(arrived))
                span = STEP_SPAN + ADD_SPAN * count * (high - low) / 1024
                actions.append((("a", batch, number, index), needed, span, made))
    every = (PAIR, PAIR, slice(0, PLANES))
    for batch in range(micro_count):
        before = [("d", batch - 1, group, side) for group in range(len(GROUPS)) for side in (0, 1)]
        before = before if batch else []
        for group in range(len(GROUPS)):
            numbers = group_streams(group)
            share = sum(streams[number][1] - streams[number][0] for number in numbers) / width
            for side in (0, 1):
                needed = [
                    ("g", batch, number, name)
                    for number in numbers
                    for name, hop, _, _ in gather_messages(streams[number][2])
                    if (hop == CORE) == bool(side)
                ]
                for piece in range(len(ups)):
                    earlier = [("u", batch, group - 1, side, piece)] if group else before
                    span = UP_SPAN * share / len(ups)
                    actions.append((("u", batch, group, side, piece), needed + earlier, span, []))
        done = [
            ("u", batch, len(GROUPS) - 1, side, piece) for side in (0, 1) for piece in range(len(ups))
        ]
        for group in range(len(GROUPS)):
            numbers = group_streams(group)
            share = sum(streams[number][1] - streams[number][0] for number in numbers) / width
            for side in (1, 0):
                made = [
                    (("r", batch, number, "c"), CORE, every) + streams[number][:2]
                    for number in numbers
                    if side
                ]
                actions.append((("d", batch, group, side), done, DOWN_START + DOWN_SPAN * share, made))
                done = done + [("d", batch, group, side)]
    return actions


def plan_actions(actions, tokens):
    moment, ready_at, link_free, order = 0.0, {}, {}, []
    left = sorted(
        actions,
        key=lambda action: (PREFERENCE[action[0][:2]], {"s": 1, "a": 0}.get(action[0][0], 0) * action[0][2]),
    )
    while left:
        best = None
        for action in left:
            if all(need in ready_at for need in action[1]):
                start = max([ready_at[need] for need in action[1]], default=0.0)
                if start <= moment:
                    best = (moment, action)
                    break
                if best is None or start < best[0]:
                    best = (start, action)
        start, action = best
        left.remove(action)
        order.append(action)
        moment = max(moment, start) + action[2] + SEND_SPAN * len(action[3])
        ready_at[action[0]] = moment
        for label, hop, rows, low, high in action[3]:
            span = 2 * len(rows_of(rows)) * tokens * (high - low)
            span = span / (CORE_RATE if hop == CORE else LINK_RATE) + MESSAGE_SPAN
            used, delay = LINKS[hop]
            for link, times in used:
                link_free[link] = max(link_free.get(link, 0.0), moment) + span * times
            ready_at[label] = max(link_free[link] for link, _ in used) + delay
    return order, moment


def tree_kernel(
    hidden_ref,
    gain_ref,
    ids_ref,
    weight_ref,
    gate_hbm,
    up_hbm,
    down_hbm,
    out_ref,
    rows,
    parts,
    arrived,
    gate_w,
    up_w,
    down_w,
    act,
    gate_part,
    up_part,
    weight_sems,
    send_sem,
    recv_sems,
    sent,
):
    micro_count, tokens, model_width = hidden_ref.shape
    width = rows.shape[-1]
    devices = lax.axis_size("req")
    half = devices // 2
    me = lax.axis_index("req")
    experts = devices // HSPLIT
    expert = me // HSPLIT
    streams = lane_streams(width)
    hops = [CORE, X, Y] + [plane * Z for plane in range(1, PLANES)]

    def across(hop):
        if hop < Z:
            return me + (1 - 2 * ((me // hop) % 2)) * hop
        plane, flips = me // Z, hop // Z
        low = plane % 2 + (flips % 2) * (1 - 2 * (plane % 2))
        high = plane // 2 + (flips // 2) * (1 - 2 * (plane // 2))
        return me % Z + Z * (2 * high + low)

    partner = {hop: across(hop) for hop in hops}
    barrier = pltpu.get_barrier_semaphore()
    for hop in hops:
        pl.semaphore_signal(
            barrier, inc=1, device_id={"req": partner[hop]}, device_id_type=pl.DeviceIdType.MESH
        )
    loads = [
        pltpu.make_async_copy(source, target, weight_sems.at[number])
        for number, (source, target) in enumerate(
            ((gate_hbm, gate_w), (up_hbm, up_w), (down_hbm, down_w))
        )
    ]
    for load in loads:
        load.start()

    tail = width - model_width
    lane_of = lax.broadcasted_iota(jnp.int32, (1, tail), 1)
    line_of = lax.broadcasted_iota(jnp.int32, (tail, 1), 0)
    named = line_of - experts * (line_of // experts)
    gain = gain_ref[...].astype(jnp.float32)[None, :]
    for batch in range(micro_count):
        residual = hidden_ref[batch].astype(jnp.float32)
        scale = lax.rsqrt(jnp.mean(residual * residual, axis=-1, keepdims=True) + epsilon)
        rows[batch, 0, 0, 0, 0, :, :model_width] = (residual * scale * gain).astype(jnp.bfloat16)
        table = jnp.zeros((tail, tokens), jnp.float32)
        for member in range(ids_ref.shape[1]):
            table = table + jnp.where(
                ids_ref[batch, member : member + 1, :] == named,
                weight_ref[batch, member : member + 1, :],
                0.0,
            )
        table = table.T
        upper = table.astype(jnp.bfloat16).astype(jnp.float32)
        shown = jnp.where(lane_of < experts, upper, table - upper)
        shown = jnp.where(lane_of < 2 * experts, shown, 0.0)
        rows[batch, 0, 0, 0, 0, :, model_width:] = shown.astype(jnp.bfloat16)
    pl.semaphore_wait(barrier, len(hops))

    slots = {}
    waits = {}

    def remote(source, target, label, hop):
        kind, batch, number, name = label
        low, high, order = streams[number]
        taken = together(label, order)
        key = label if taken is None else label[:3] + taken[0]
        slot = slots.setdefault(key, len(slots))
        copy = pltpu.make_async_remote_copy(
            src_ref=source,
            dst_ref=target,
            send_sem=send_sem,
            recv_sem=recv_sems.at[slot],
            device_id={"req": partner[hop]},
            device_id_type=pl.DeviceIdType.MESH,
        )
        if taken is None:
            waits[label] = (key, copy.wait_recv)
        else:
            xs, ys, zs = taken[1]
            whole = (rows if kind == "g" else arrived).at[batch, 0, xs, ys, zs, :, low:high]
            waits[label] = (key, pltpu.make_async_copy(whole, whole, recv_sems.at[slot]).wait)
        return copy

    copies = {}
    for batch in range(micro_count):
        for number, (low, high, order) in enumerate(streams):
            lanes = slice(low, high)
            for name, hop, (xs, ys, zs), _ in gather_messages(order):
                flip = lambda part, bit: one(part.start ^ 1) if hop == bit else part
                landing = (flip(xs, X), flip(ys, Y), zs)
                if hop >= Z:
                    landing = (xs, ys, one(zs.start ^ (hop // Z)))
                side = 1 if hop == CORE else 0
                label = ("g", batch, number, name)
                copies[label] = remote(
                    rows.at[batch, 0, xs, ys, zs, :, lanes],
                    rows.at[(batch, side) + landing + (slice(None), lanes)],
                    label,
                    hop,
                )
            label = ("r", batch, number, "c")
            copies[label] = remote(
                parts.at[batch, 1, :, :, :, :, lanes],
                arrived.at[batch, 1, :, :, :, :, lanes],
                label,
                CORE,
            )
            for _, sends, _ in reduce_steps(order):
                for name, hop, (xs, ys, zs) in sends:
                    label = ("r", batch, number, name)
                    copies[label] = remote(
                        parts.at[batch, 0, xs, ys, zs, :, lanes],
                        arrived.at[batch, 0, xs, ys, zs, :, lanes],
                        label,
                        hop,
                    )

    chosen = (lane_of == expert) | (lane_of == experts + expert)
    hidden_units = gate_w.shape[0]
    ups = lane_pieces(0, hidden_units, 256)
    rowwise = (((1,), (1,)), ((), ()))

    def up_piece(batch, group, side, piece):
        low, high = ups[piece]
        numbers = group_streams(group)
        start, stop = streams[numbers[0]][0], min(streams[numbers[-1]][1], model_width)
        slab = rows[batch, side, :, :, :, :, start:stop].reshape(half * tokens, stop - start)
        gate = lax.dot_general(
            slab, gate_w[low:high, start:stop], rowwise, preferred_element_type=jnp.float32
        )
        upward = lax.dot_general(
            slab, up_w[low:high, start:stop], rowwise, preferred_element_type=jnp.float32
        )
        if group:
            gate = gate_part[side, :, low:high] + gate
            upward = up_part[side, :, low:high] + upward
        if group < len(GROUPS) - 1:
            gate_part[side, :, low:high] = gate
            up_part[side, :, low:high] = upward
        else:
            ends = rows[batch, side, :, :, :, :, model_width:].reshape(half * tokens, tail)
            weight = jnp.sum(
                jnp.where(chosen, ends.astype(jnp.float32), 0.0), axis=1, keepdims=True
            )
            act[side, :, low:high] = (
                weight * ((upward + 1.0) * gate * jax.nn.sigmoid(swish_scale * gate))
            ).astype(jnp.bfloat16)

    def down_piece(batch, group, side):
        numbers = group_streams(group)
        low, high = streams[numbers[0]][0], min(streams[numbers[-1]][1], model_width)
        for start, stop in lane_pieces(low, high, 512):
            part = jnp.dot(
                act[side], down_w[:, start:stop], preferred_element_type=jnp.float32
            )
            parts[batch, side, :, :, :, :, start:stop] = (
                part.astype(parts.dtype).reshape(2, 2, PLANES, tokens, stop - start)
            )

    def reduce_piece(batch, number, index):
        low, high, order = streams[number]
        target, sends, others = reduce_steps(order)[index]
        stop = high if sends else min(high, model_width)
        held = rows_of(target)
        for place, (x, y, z) in enumerate(held):
            total = parts[batch, 0, x, y, z, :, low:stop].astype(jnp.float32)
            if not sends:
                total = total + hidden_ref[batch, :, low:stop].astype(jnp.float32)
            total = total + arrived[batch, 1, x, y, z, :, low:stop].astype(jnp.float32)
            for _, block_rows in others:
                inside = rows_of(block_rows)
                matching = inside if len(held) == 1 else [inside[place]]
                for ox, oy, oz in matching:
                    total = total + arrived[batch, 0, ox, oy, oz, :, low:stop].astype(jnp.float32)
            if sends:
                parts[batch, 0, x, y, z, :, low:stop] = total.astype(parts.dtype)
            else:
                out_ref[batch, :, low:stop] = total.astype(out_ref.dtype)

    parts[:, :, :, :, :, :, model_width:] = jnp.zeros(parts.shape[:-1] + (tail,), parts.dtype)
    landed, loaded = set(), set()
    actions = all_actions(micro_count, tokens, width, ups)
    for key, needs, _, sends in plan_actions(actions, tokens)[0]:
        for need in needs:
            if need in waits and waits[need][0] not in landed:
                landed.add(waits[need][0])
                waits[need][1]()
        kind = key[0]
        if kind == "u":
            if kind not in loaded:
                loads[0].wait()
                loads[1].wait()
            up_piece(*key[1:])
        elif kind == "d":
            if kind not in loaded:
                loads[2].wait()
            down_piece(*key[1:])
        elif kind == "a":
            reduce_piece(*key[1:])
        loaded.add(kind)
        for label, *_ in sends:
            copies[label].start()
    pltpu.make_async_copy(sent, sent, send_sem).wait()


def tree_local(hidden, norm_gain, w_gate, w_up, w_down, expert_ids, route_weight):
    micro_count, tokens, model_width = hidden.shape
    devices = lax.axis_size("req")
    width = padded(model_width)
    hidden_units = w_gate.shape[1]
    vmem = pl.BlockSpec(memory_space=pltpu.VMEM)
    hbm = pl.BlockSpec(memory_space=pl.ANY)
    slots = (micro_count, 2, 2, 2, PLANES, tokens, width)
    labels = [
        (kind, batch, number, name)
        for batch in range(micro_count)
        for number, (_, _, order) in enumerate(lane_streams(width))
        for kind, names in (
            ("g", [message[0] for message in gather_messages(order)]),
            ("r", ["c"] + [name for step in reduce_steps(order) for name, _, _ in step[1]]),
        )
        for name in names
    ]
    orders = [order for _, _, order in lane_streams(width)]
    grouped = [together(label, orders[label[2]]) for label in labels]
    messages = len(
        {
            label if taken is None else label[:3] + taken[0]
            for label, taken in zip(labels, grouped)
        }
    )
    return pl.pallas_call(
        tree_kernel,
        out_shape=jax.ShapeDtypeStruct(hidden.shape, hidden.dtype),
        in_specs=[vmem, vmem, vmem, vmem, hbm, hbm, hbm],
        out_specs=vmem,
        scratch_shapes=[
            pltpu.VMEM(slots, jnp.bfloat16),
            pltpu.VMEM(slots, jnp.bfloat16),
            pltpu.VMEM(slots, jnp.bfloat16),
            pltpu.VMEM((hidden_units, model_width), w_gate.dtype),
            pltpu.VMEM((hidden_units, model_width), w_up.dtype),
            pltpu.VMEM((hidden_units, model_width), w_down.dtype),
            pltpu.VMEM((2, devices // 2 * tokens, hidden_units), jnp.bfloat16),
            pltpu.VMEM((2, devices // 2 * tokens, hidden_units), jnp.float32),
            pltpu.VMEM((2, devices // 2 * tokens, hidden_units), jnp.float32),
            pltpu.SemaphoreType.DMA((3,)),
            pltpu.SemaphoreType.DMA,
            pltpu.SemaphoreType.DMA((messages,)),
            pltpu.VMEM((2 * micro_count * (devices - 1), tokens, width), jnp.bfloat16),
        ],
        compiler_params=pltpu.CompilerParams(
            collective_id=0, has_side_effects=True, vmem_limit_bytes=VMEM_BYTES
        ),
        name="tree",
    )(
        hidden,
        norm_gain,
        expert_ids.transpose(0, 2, 1),
        route_weight.transpose(0, 2, 1),
        w_gate.T,
        w_up.T,
        w_down,
    )


def tree_fits(hidden, norm_gain, w_gate, w_up, w_down, expert_ids, route_weight):
    micro_count, tokens, model_width = hidden.shape
    devices = lax.axis_size("req")
    width = padded(model_width)
    units = w_gate.shape[1]
    slots = 3 * micro_count * devices * tokens * width
    weights = 3 * units * width
    work = 3 * devices * tokens * width
    return (
        devices == 8 * PLANES
        and 2 * (devices // HSPLIT) <= width - model_width
        and 2 * (slots + weights + work) <= VMEM_BYTES
    )


def local(*arguments):
    return (tree_local if tree_fits(*arguments) else routed_local)(*arguments)


def solution(mesh):
    return jax.shard_map(
        local,
        mesh=mesh,
        in_specs=(
            P(None, ("groups", "req"), None),
            P(),
            P(None, "req"),
            P(None, "req"),
            P("req", None),
            P(None, ("groups", "req"), None),
            P(None, ("groups", "req"), None),
        ),
        out_specs=P(None, ("groups", "req"), None),
        check_vma=False,
    )
```

```python
import functools

import jax
import jax.numpy as jnp
from jax import lax
from jax.experimental import pallas as pl
from jax.experimental.pallas import tpu as pltpu
from jax.sharding import PartitionSpec as P

HSPLIT = 4


epsilon = 1e-05
swish_scale = 1.702


def swapped(block, axis, apart):
    count = lax.axis_size(axis)
    route = []
    for low in range(count):
        high = low | 1 << apart
        if high != low and high < count:
            route += [(low, high), (high, low)]
    return lax.ppermute(block, axis, route)


def routed_local(hidden, norm_gain, w_gate, w_up, w_down, expert_ids, route_weight):
    micro_count, tokens, model_width = hidden.shape
    top_count = expert_ids.shape[2]
    devices = lax.axis_size("req")
    experts = devices // HSPLIT
    rounded = HSPLIT * (
        (3 * tokens * top_count + 2 * experts * HSPLIT - 1) // (2 * experts * HSPLIT)
    )
    capacity = min(tokens, max(HSPLIT, rounded))
    quarter = capacity // HSPLIT
    levels = HSPLIT.bit_length() - 1
    position = lax.axis_index("req")
    gain_f32 = norm_gain.astype(jnp.float32)
    results = []
    for batch_index in range(micro_count):
        residual = hidden[batch_index].astype(jnp.float32)
        normed = (
            residual
            * lax.rsqrt(jnp.mean(residual * residual, axis=-1, keepdims=True) + epsilon)
            * gain_f32
        ).astype(jnp.bfloat16)
        flat_ids = expert_ids[batch_index].reshape(-1)
        onehot = (flat_ids[:, None] == jnp.arange(experts, dtype=jnp.int32)[None, :]).astype(
            jnp.int32
        )
        slot_index = jnp.sum((jnp.cumsum(onehot, axis=0) - onehot) * onehot, axis=1)
        target = flat_ids * capacity + slot_index
        placing = (
            target[:, None] == jnp.arange(experts * capacity, dtype=jnp.int32)[None, :]
        ).reshape(tokens, top_count, experts * capacity)
        selector = jnp.any(placing, axis=1).astype(jnp.bfloat16)
        outgoing = jnp.dot(selector.T, normed, preferred_element_type=jnp.float32).astype(
            jnp.bfloat16
        )
        copies = jnp.broadcast_to(
            outgoing.reshape(experts, 1, capacity, model_width),
            (experts, HSPLIT, capacity, model_width),
        ).reshape(devices, capacity, model_width)
        received = lax.all_to_all(copies, "req", split_axis=0, concat_axis=0, tiled=True)
        count = received.shape[1]
        slot_rows = received.reshape(-1, model_width)
        gate = jnp.dot(slot_rows, w_gate, preferred_element_type=jnp.float32)
        upward = jnp.dot(slot_rows, w_up, preferred_element_type=jnp.float32)
        act = ((upward + 1.0) * gate * jax.nn.sigmoid(swish_scale * gate)).astype(jnp.bfloat16)
        source_form = jnp.dot(act, w_down, preferred_element_type=jnp.float32).reshape(
            devices, count, model_width
        )
        shard_form = source_form.reshape(devices, HSPLIT, quarter, model_width).transpose(
            1, 0, 2, 3
        )
        folded = shard_form
        for bit_index in reversed(range(levels)):
            halfway = folded.shape[0] // 2
            upper_side = position >> bit_index & 1 == 1
            kept_part = jnp.where(upper_side, folded[halfway:], folded[:halfway])
            given_part = jnp.where(upper_side, folded[:halfway], folded[halfway:])
            folded = kept_part + swapped(given_part, "req", bit_index)
        own_rows = folded[0].astype(jnp.bfloat16)
        expert_out = lax.all_to_all(
            own_rows, "req", split_axis=0, concat_axis=0, tiled=True
        ).reshape(experts * capacity, model_width)
        weigh_table = jnp.sum(
            placing.astype(jnp.float32) * route_weight[batch_index][:, :, None], axis=1
        )
        mixture = jnp.dot(
            weigh_table, expert_out.astype(jnp.float32), precision=lax.Precision.HIGHEST
        )
        results.append((residual + mixture).astype(jnp.bfloat16))
    return jnp.stack(results, axis=0)

LANES = 128
PLANES = 4
CORE, X, Y, Z = 1, 2, 4, 8
GROUPS = (
    ((6, "zxy"), (4, "zyx")),
    ((5, "yxz"), (3, "zyx")),
    ((5, "zxy"),),
)
PREFERENCE = {
    ("s", 0): 0,
    ("s", 1): 2,
    ("a", 0): 0,
    ("a", 1): 1,
    ("u", 0): 4,
    ("u", 1): 5,
    ("d", 0): 3,
    ("d", 1): 6,
}
SHARES = tuple(stream for members in GROUPS for stream in members)
HELD = 3
VMEM_BYTES = 60 * 1024 * 1024
LINK_RATE, CORE_RATE = 49.5e3, 1400e3
LINKS = {
    CORE: (((CORE, 1),), 1.12),
    X: (((X, 1),), 1.92),
    Y: (((Y, 1),), 1.92),
    Z: (((Z, 1),), 1.92),
    2 * Z: (((Z, 1), (2 * Z, 2)), 2.72),
    3 * Z: (((Z, 1), (2 * Z, 2)), 3.47),
}
UP_SPAN, DOWN_SPAN, DOWN_START, ADD_SPAN = 2.58, 1.33, 0.08, 0.0144
STEP_SPAN, SEND_SPAN, MESSAGE_SPAN = 0.092, 0.023, 0.034
ROW = slice(0, 1)
PAIR = slice(0, 2)


def padded(size):
    return -(-size // LANES) * LANES


def lane_streams(width):
    tiles, total, low, streams = width // LANES, sum(share for share, _ in SHARES), 0, []
    for number, (share, order) in enumerate(SHARES):
        taken = sum(part for part, _ in SHARES[: number + 1])
        high = tiles * taken // total * LANES
        streams.append((low, high, order))
        low = high
    return streams


def one(value):
    return slice(value, value + 1)


def block(order, first, second, depth):
    return (first, second, depth) if order == "zyx" else (second, first, depth)


def gather_messages(order):
    every, later = slice(0, PLANES), slice(1, PLANES)
    own = (ROW, ROW, ROW)
    messages = []
    if order == "yxz":
        square = (PAIR, PAIR, ROW)
        messages += [
            ("y0", Y, own, ()),
            ("x0", X, own, ()),
            ("xy", X, (ROW, one(1), ROW), ("y0",)),
            ("z2", 2 * Z, square, ("x0", "xy")),
            ("z1", Z, square, ("x0", "xy")),
            ("z3", Z, (PAIR, PAIR, one(2)), ("z2",)),
            ("c", CORE, (PAIR, PAIR, every), ("x0", "xy", "z1", "z2", "z3")),
        ]
        return messages
    far, near = (X, Y) if order == "zyx" else (Y, X)
    planes = tuple("z%d" % plane for plane in range(1, PLANES))
    messages += [("z%d" % plane, plane * Z, own, ()) for plane in range(1, PLANES)]
    messages += [
        ("n0", near, own, ()),
        ("f0", far, own, ()),
        ("nz", near, (ROW, ROW, later), planes),
        ("fz", far, (ROW, ROW, later), planes),
        ("fn", far, block(order, ROW, one(1), ROW), ("n0",)),
        ("fnz", far, block(order, ROW, one(1), later), ("nz",)),
        ("c", CORE, (PAIR, PAIR, every), ("f0", "fz", "fn", "fnz")),
    ]
    return messages


def reduce_steps(order):
    every, later = slice(0, PLANES), slice(1, PLANES)
    own = (ROW, ROW, ROW)
    if order == "yxz":
        at = lambda plane: (PAIR, PAIR, one(plane))
        return [
            (at(3), [("z3", Z, at(3))], []),
            (at(1), [("z1", Z, at(1))], []),
            (at(2), [("z2", 2 * Z, at(2))], [("z3", at(3))]),
            (
                (one(1), PAIR, ROW),
                [("x", X, (one(1), PAIR, ROW))],
                [("z1", (one(1), PAIR, one(1))), ("z2", (one(1), PAIR, one(2)))],
            ),
            (
                (ROW, one(1), ROW),
                [("y", Y, (ROW, one(1), ROW))],
                [
                    ("z1", (ROW, one(1), one(1))),
                    ("z2", (ROW, one(1), one(2))),
                    ("x", (one(1), one(1), ROW)),
                ],
            ),
            (
                own,
                [],
                [
                    ("z1", (ROW, ROW, one(1))),
                    ("z2", (ROW, ROW, one(2))),
                    ("x", (one(1), ROW, ROW)),
                    ("y", (ROW, one(1), ROW)),
                ],
            ),
        ]
    far, near = (X, Y) if order == "zyx" else (Y, X)
    at = functools.partial(block, order)
    corner, side, face = at(one(1), one(1), every), at(one(1), ROW, every), at(ROW, one(1), every)
    planes = [(ROW, ROW, one(plane)) for plane in range(1, PLANES)]
    names = ["z%d" % plane for plane in range(1, PLANES)]
    return [
        (corner, [("fn", far, corner)], []),
        (side, [("f", far, side)], []),
        (face, [("n", near, face)], [("fn", corner)]),
        (
            (ROW, ROW, later),
            [(name, plane * Z, planes[plane - 1]) for plane, name in enumerate(names, 1)],
            [("f", at(one(1), ROW, later)), ("n", at(ROW, one(1), later))],
        ),
        (
            own,
            [],
            [("f", at(one(1), ROW, ROW)), ("n", at(ROW, one(1), ROW))] + list(zip(names, planes)),
        ),
    ]


def together(label, order):
    kind, _, _, name = label
    planes = ("z1", "z2", "z3")
    if order != "yxz" and name in planes:
        return planes, (ROW, ROW, slice(1, PLANES))
    if kind == "g" and order == "yxz" and name in ("x0", "xy"):
        return ("x0", "xy"), (one(1), PAIR, ROW)
    if kind == "g" and order != "yxz" and name in ("f0", "fz", "fn", "fnz"):
        return ("f0", "fz", "fn", "fnz"), block(order, one(1), PAIR, slice(0, PLANES))
    return None


def rows_of(rows):
    return [
        (x, y, z)
        for x in range(rows[0].start, rows[0].stop)
        for y in range(rows[1].start, rows[1].stop)
        for z in range(rows[2].start, rows[2].stop)
    ]


def lane_pieces(low, high, size):
    return [(start, min(high, start + size)) for start in range(low, high, size)]


def group_streams(group):
    first = sum(len(members) for members in GROUPS[:group])
    return range(first, first + len(GROUPS[group]))


def all_actions(micro_count, tokens, width, ups):
    streams = lane_streams(width)
    whole = 2 * PLANES * 4 * tokens
    actions = []
    for batch in range(micro_count):
        for number, (low, high, order) in enumerate(streams):
            for name, hop, rows, needs in gather_messages(order):
                needed = [("g", batch, number, need) for need in needs]
                if batch and not needs:
                    needed = [("s", batch - 1, HELD, gather_messages(streams[HELD][2])[-2][0])]
                made = [(("g", batch, number, name), hop, rows, low, high)]
                actions.append((("s", batch, number, name), needed, STEP_SPAN, made))
    for batch in range(micro_count):
        for number, (low, high, order) in enumerate(streams):
            group = [number in group_streams(index) for index in range(len(GROUPS))].index(True)
            for index, (rows, sends, arrived) in enumerate(reduce_steps(order)):
                needed = [("d", batch, group, 0), ("r", batch, number, "c")]
                needed += [("r", batch, number, name) for name, _ in arrived]
                made = [
                    (("r", batch, number, name), hop, sent, low, high) for name, hop, sent in sends
                ]
                count = len(rows_of(rows)) * (2 + len(arrived))
                span = STEP_SPAN + ADD_SPAN * count * (high - low) / 1024
                actions.append((("a", batch, number, index), needed, span, made))
    every = (PAIR, PAIR, slice(0, PLANES))
    for batch in range(micro_count):
        before = [("d", batch - 1, group, side) for group in range(len(GROUPS)) for side in (0, 1)]
        before = before if batch else []
        for group in range(len(GROUPS)):
            numbers = group_streams(group)
            share = sum(streams[number][1] - streams[number][0] for number in numbers) / width
            for side in (0, 1):
                needed = [
                    ("g", batch, number, name)
                    for number in numbers
                    for name, hop, _, _ in gather_messages(streams[number][2])
                    if (hop == CORE) == bool(side)
                ]
                for piece in range(len(ups)):
                    earlier = [("u", batch, group - 1, side, piece)] if group else before
                    span = UP_SPAN * share / len(ups)
                    actions.append((("u", batch, group, side, piece), needed + earlier, span, []))
        done = [
            ("u", batch, len(GROUPS) - 1, side, piece) for side in (0, 1) for piece in range(len(ups))
        ]
        for group in range(len(GROUPS)):
            numbers = group_streams(group)
            share = sum(streams[number][1] - streams[number][0] for number in numbers) / width
            for side in (1, 0):
                made = [
                    (("r", batch, number, "c"), CORE, every) + streams[number][:2]
                    for number in numbers
                    if side
                ]
                actions.append((("d", batch, group, side), done, DOWN_START + DOWN_SPAN * share, made))
                done = done + [("d", batch, group, side)]
    return actions


def plan_actions(actions, tokens):
    moment, ready_at, link_free, order = 0.0, {}, {}, []
    left = sorted(
        actions,
        key=lambda action: (PREFERENCE[action[0][:2]], {"s": 1, "a": 0}.get(action[0][0], 0) * action[0][2]),
    )
    while left:
        best = None
        for action in left:
            if all(need in ready_at for need in action[1]):
                start = max([ready_at[need] for need in action[1]], default=0.0)
                if start <= moment:
                    best = (moment, action)
                    break
                if best is None or start < best[0]:
                    best = (start, action)
        start, action = best
        left.remove(action)
        order.append(action)
        moment = max(moment, start) + action[2] + SEND_SPAN * len(action[3])
        ready_at[action[0]] = moment
        for label, hop, rows, low, high in action[3]:
            span = 2 * len(rows_of(rows)) * tokens * (high - low)
            span = span / (CORE_RATE if hop == CORE else LINK_RATE) + MESSAGE_SPAN
            used, delay = LINKS[hop]
            for link, times in used:
                link_free[link] = max(link_free.get(link, 0.0), moment) + span * times
            ready_at[label] = max(link_free[link] for link, _ in used) + delay
    return order, moment


def tree_kernel(
    hidden_ref,
    gain_ref,
    ids_ref,
    weight_ref,
    gate_hbm,
    up_hbm,
    down_hbm,
    out_ref,
    rows,
    parts,
    arrived,
    gate_w,
    up_w,
    down_w,
    act,
    gate_part,
    up_part,
    scale_part,
    weight_sems,
    send_sem,
    recv_sems,
    sent,
):
    micro_count, tokens, model_width = hidden_ref.shape
    width = rows.shape[-1]
    devices = lax.axis_size("req")
    half = devices // 2
    me = lax.axis_index("req")
    experts = devices // HSPLIT
    expert = me // HSPLIT
    streams = lane_streams(width)
    hops = [CORE, X, Y] + [plane * Z for plane in range(1, PLANES)]

    def across(hop):
        if hop < Z:
            return me + (1 - 2 * ((me // hop) % 2)) * hop
        plane, flips = me // Z, hop // Z
        low = plane % 2 + (flips % 2) * (1 - 2 * (plane % 2))
        high = plane // 2 + (flips // 2) * (1 - 2 * (plane // 2))
        return me % Z + Z * (2 * high + low)

    partner = {hop: across(hop) for hop in hops}
    barrier = pltpu.get_barrier_semaphore()
    for hop in hops:
        pl.semaphore_signal(
            barrier, inc=1, device_id={"req": partner[hop]}, device_id_type=pl.DeviceIdType.MESH
        )
    loads = [
        pltpu.make_async_copy(source, target, weight_sems.at[number])
        for number, (source, target) in enumerate(
            ((gate_hbm, gate_w), (up_hbm, up_w), (down_hbm, down_w))
        )
    ]
    for load in loads:
        load.start()

    tail = width - model_width
    lane_of = lax.broadcasted_iota(jnp.int32, (1, tail), 1)
    line_of = lax.broadcasted_iota(jnp.int32, (tail, 1), 0)
    named = line_of - experts * (line_of // experts)
    gain = gain_ref[...].astype(jnp.float32)[None, :]
    for batch in range(micro_count):
        residual = hidden_ref[batch].astype(jnp.float32)
        scale = lax.rsqrt(jnp.mean(residual * residual, axis=-1, keepdims=True) + epsilon)
        rows[batch, 0, 0, 0, 0, :, :model_width] = (residual * scale * gain).astype(jnp.bfloat16)
        table = jnp.zeros((tail, tokens), jnp.float32)
        for member in range(ids_ref.shape[1]):
            table = table + jnp.where(
                ids_ref[batch, member : member + 1, :] == named,
                weight_ref[batch, member : member + 1, :],
                0.0,
            )
        table = table.T
        upper = table.astype(jnp.bfloat16).astype(jnp.float32)
        shown = jnp.where(lane_of < experts, upper, table - upper)
        shown = jnp.where(lane_of < 2 * experts, shown, 0.0)
        rows[batch, 0, 0, 0, 0, :, model_width:] = shown.astype(jnp.bfloat16)
    pl.semaphore_wait(barrier, len(hops))

    slots = {}
    waits = {}

    def remote(source, target, label, hop):
        kind, batch, number, name = label
        low, high, order = streams[number]
        taken = together(label, order)
        key = label if taken is None else label[:3] + taken[0]
        slot = slots.setdefault(key, len(slots))
        copy = pltpu.make_async_remote_copy(
            src_ref=source,
            dst_ref=target,
            send_sem=send_sem,
            recv_sem=recv_sems.at[slot],
            device_id={"req": partner[hop]},
            device_id_type=pl.DeviceIdType.MESH,
        )
        if taken is None:
            waits[label] = (key, copy.wait_recv)
        else:
            xs, ys, zs = taken[1]
            whole = (rows if kind == "g" else arrived).at[batch, 0, xs, ys, zs, :, low:high]
            waits[label] = (key, pltpu.make_async_copy(whole, whole, recv_sems.at[slot]).wait)
        return copy

    copies = {}
    for batch in range(micro_count):
        for number, (low, high, order) in enumerate(streams):
            lanes = slice(low, high)
            for name, hop, (xs, ys, zs), _ in gather_messages(order):
                flip = lambda part, bit: one(part.start ^ 1) if hop == bit else part
                landing = (flip(xs, X), flip(ys, Y), zs)
                if hop >= Z:
                    landing = (xs, ys, one(zs.start ^ (hop // Z)))
                side = 1 if hop == CORE else 0
                label = ("g", batch, number, name)
                copies[label] = remote(
                    rows.at[batch, 0, xs, ys, zs, :, lanes],
                    rows.at[(batch, side) + landing + (slice(None), lanes)],
                    label,
                    hop,
                )
            label = ("r", batch, number, "c")
            copies[label] = remote(
                parts.at[batch, 1, :, :, :, :, lanes],
                arrived.at[batch, 1, :, :, :, :, lanes],
                label,
                CORE,
            )
            for _, sends, _ in reduce_steps(order):
                for name, hop, (xs, ys, zs) in sends:
                    label = ("r", batch, number, name)
                    copies[label] = remote(
                        parts.at[batch, 0, xs, ys, zs, :, lanes],
                        arrived.at[batch, 0, xs, ys, zs, :, lanes],
                        label,
                        hop,
                    )

    chosen = (lane_of == expert) | (lane_of == experts + expert)
    hidden_units = gate_w.shape[0]
    ups = lane_pieces(0, hidden_units, 256)
    rowwise = (((1,), (1,)), ((), ()))
    scaled = set()

    def up_piece(batch, group, side, piece):
        low, high = ups[piece]
        numbers = group_streams(group)
        start, stop = streams[numbers[0]][0], min(streams[numbers[-1]][1], model_width)
        slab = rows[batch, side, :, :, :, :, start:stop].reshape(half * tokens, stop - start)
        gate = lax.dot_general(
            slab, gate_w[low:high, start:stop], rowwise, preferred_element_type=jnp.float32
        )
        upward = lax.dot_general(
            slab, up_w[low:high, start:stop], rowwise, preferred_element_type=jnp.float32
        )
        if group:
            gate = gate_part[side, :, low:high] + gate
            upward = up_part[side, :, low:high] + upward
        if group < len(GROUPS) - 1:
            gate_part[side, :, low:high] = gate
            up_part[side, :, low:high] = upward
        else:
            if (batch, side) not in scaled:
                scaled.add((batch, side))
                ends = rows[batch, side, :, :, :, :, model_width:].reshape(half * tokens, tail)
                total = jnp.sum(
                    jnp.where(chosen, ends.astype(jnp.float32), 0.0), axis=1, keepdims=True
                )
                scale_part[side] = jnp.broadcast_to(total, scale_part.shape[1:])
            copies_wide = -(-(high - low) // LANES)
            weight = jnp.concatenate([scale_part[side]] * copies_wide, axis=1)[:, : high - low]
            act[side, :, low:high] = (
                weight * ((upward + 1.0) * gate * jax.nn.sigmoid(swish_scale * gate))
            ).astype(jnp.bfloat16)

    def down_piece(batch, group, side):
        numbers = group_streams(group)
        low, high = streams[numbers[0]][0], min(streams[numbers[-1]][1], model_width)
        for start, stop in lane_pieces(low, high, 512):
            part = jnp.dot(
                act[side], down_w[:, start:stop], preferred_element_type=jnp.float32
            )
            parts[batch, side, :, :, :, :, start:stop] = (
                part.astype(parts.dtype).reshape(2, 2, PLANES, tokens, stop - start)
            )

    def reduce_piece(batch, number, index):
        low, high, order = streams[number]
        target, sends, others = reduce_steps(order)[index]
        stop = high if sends else min(high, model_width)
        held = rows_of(target)
        for place, (x, y, z) in enumerate(held):
            total = parts[batch, 0, x, y, z, :, low:stop].astype(jnp.float32)
            if not sends:
                total = total + hidden_ref[batch, :, low:stop].astype(jnp.float32)
            total = total + arrived[batch, 1, x, y, z, :, low:stop].astype(jnp.float32)
            for _, block_rows in others:
                inside = rows_of(block_rows)
                matching = inside if len(held) == 1 else [inside[place]]
                for ox, oy, oz in matching:
                    total = total + arrived[batch, 0, ox, oy, oz, :, low:stop].astype(jnp.float32)
            if sends:
                parts[batch, 0, x, y, z, :, low:stop] = total.astype(parts.dtype)
            else:
                out_ref[batch, :, low:stop] = total.astype(out_ref.dtype)

    parts[:, :, :, :, :, :, model_width:] = jnp.zeros(parts.shape[:-1] + (tail,), parts.dtype)
    landed, loaded = set(), set()
    actions = all_actions(micro_count, tokens, width, ups)
    for key, needs, _, sends in plan_actions(actions, tokens)[0]:
        for need in needs:
            if need in waits and waits[need][0] not in landed:
                landed.add(waits[need][0])
                waits[need][1]()
        kind = key[0]
        if kind == "u":
            if kind not in loaded:
                loads[0].wait()
                loads[1].wait()
            up_piece(*key[1:])
        elif kind == "d":
            if kind not in loaded:
                loads[2].wait()
            down_piece(*key[1:])
        elif kind == "a":
            reduce_piece(*key[1:])
        loaded.add(kind)
        for label, *_ in sends:
            copies[label].start()
    pltpu.make_async_copy(sent, sent, send_sem).wait()


def tree_local(hidden, norm_gain, w_gate, w_up, w_down, expert_ids, route_weight):
    micro_count, tokens, model_width = hidden.shape
    devices = lax.axis_size("req")
    width = padded(model_width)
    hidden_units = w_gate.shape[1]
    vmem = pl.BlockSpec(memory_space=pltpu.VMEM)
    hbm = pl.BlockSpec(memory_space=pl.ANY)
    slots = (micro_count, 2, 2, 2, PLANES, tokens, width)
    labels = [
        (kind, batch, number, name)
        for batch in range(micro_count)
        for number, (_, _, order) in enumerate(lane_streams(width))
        for kind, names in (
            ("g", [message[0] for message in gather_messages(order)]),
            ("r", ["c"] + [name for step in reduce_steps(order) for name, _, _ in step[1]]),
        )
        for name in names
    ]
    orders = [order for _, _, order in lane_streams(width)]
    grouped = [together(label, orders[label[2]]) for label in labels]
    messages = len(
        {
            label if taken is None else label[:3] + taken[0]
            for label, taken in zip(labels, grouped)
        }
    )
    return pl.pallas_call(
        tree_kernel,
        out_shape=jax.ShapeDtypeStruct(hidden.shape, hidden.dtype),
        in_specs=[vmem, vmem, vmem, vmem, hbm, hbm, hbm],
        out_specs=vmem,
        scratch_shapes=[
            pltpu.VMEM(slots, jnp.bfloat16),
            pltpu.VMEM(slots, jnp.bfloat16),
            pltpu.VMEM(slots, jnp.bfloat16),
            pltpu.VMEM((hidden_units, model_width), w_gate.dtype),
            pltpu.VMEM((hidden_units, model_width), w_up.dtype),
            pltpu.VMEM((hidden_units, model_width), w_down.dtype),
            pltpu.VMEM((2, devices // 2 * tokens, hidden_units), jnp.bfloat16),
            pltpu.VMEM((2, devices // 2 * tokens, hidden_units), jnp.float32),
            pltpu.VMEM((2, devices // 2 * tokens, hidden_units), jnp.float32),
            pltpu.VMEM((2, devices // 2 * tokens, LANES), jnp.float32),
            pltpu.SemaphoreType.DMA((3,)),
            pltpu.SemaphoreType.DMA,
            pltpu.SemaphoreType.DMA((messages,)),
            pltpu.VMEM((2 * micro_count * (devices - 1), tokens, width), jnp.bfloat16),
        ],
        compiler_params=pltpu.CompilerParams(
            collective_id=0, has_side_effects=True, vmem_limit_bytes=VMEM_BYTES
        ),
        name="tree",
    )(
        hidden,
        norm_gain,
        expert_ids.transpose(0, 2, 1),
        route_weight.transpose(0, 2, 1),
        w_gate.T,
        w_up.T,
        w_down,
    )


def tree_fits(hidden, norm_gain, w_gate, w_up, w_down, expert_ids, route_weight):
    micro_count, tokens, model_width = hidden.shape
    devices = lax.axis_size("req")
    width = padded(model_width)
    units = w_gate.shape[1]
    slots = 3 * micro_count * devices * tokens * width
    weights = 3 * units * width
    work = 3 * devices * tokens * width
    return (
        devices == 8 * PLANES
        and 2 * (devices // HSPLIT) <= width - model_width
        and 2 * (slots + weights + work) <= VMEM_BYTES
    )


def local(*arguments):
    return (tree_local if tree_fits(*arguments) else routed_local)(*arguments)


def solution(mesh):
    return jax.shard_map(
        local,
        mesh=mesh,
        in_specs=(
            P(None, ("groups", "req"), None),
            P(),
            P(None, "req"),
            P(None, "req"),
            P("req", None),
            P(None, ("groups", "req"), None),
            P(None, ("groups", "req"), None),
        ),
        out_specs=P(None, ("groups", "req"), None),
        check_vma=False,
    )
```
